128 devices in a mesh: blk: 32 (over x, z, y_hi), quarter: 4 (over y_lo, core).
Axes of the slice: x: 4, y: 4 (y_hi: 2, y_lo: 2; y = y_hi * 2 + y_lo), z: 4, core: 2. Of those that a mesh axis runs over, the one named last changes fastest.
Arguments:
- bints: bfloat16 [256, 512, 1280], P('blk', None, 'quarter'), may hold values from -2.5 to 2.5
- occ_energy: float32 [256], replicated, may hold values from -2 to -0.5
- vir_energy: float32 [512], replicated, may hold values from 0.2 to 3
Outputs:
- gamma: float32 [256, 512, 1280], P(('blk', 'quarter'))
- vvdens: float32 [512, 512], P(('blk', 'quarter'))
The draws below stay inside these ranges and needn't reach their ends.
All inputs are finite; a program needn't handle non-finite values.
Results may differ from the reference program's by a relative error of at most 0.0016.
Values may be sent and summed in bfloat16 or wider, within the bound.
A program may use at most 128 MiB of HBM per device.

```python
import jax
import jax.numpy as jnp
from jax import lax

V = 512
NAUX = 1280
OCC_DEV = 2
CYCLE = 3
O = 256
PAIRS = 1536
N_BLK = 32
N_QUARTER = 4


def shard_levels(own_key, extent, pieces, least, high):
    gain = 1.0
    for dim, parts in pieces:
        heights = jax.random.uniform(jax.random.fold_in(jax.random.fold_in(own_key, 6), dim), (parts,), jnp.float32, least / len(pieces), high / len(pieces))
        gain = gain * jnp.repeat(jnp.exp(heights), extent[dim] // parts).reshape((-1,) + (1,) * (len(extent) - 1 - dim))
    return gain


def noise(rng, shape, width, most, split=(), kind=jnp.bfloat16):
    array = width * jax.random.normal(rng, shape, jnp.float32)
    if split:
        array = array * shard_levels(rng, shape, split, -0.22, 0.18)
    return jnp.clip(array, -most, most).astype(kind)


def setup_inputs(seed: int = 0) -> dict:
    splits = jax.random.split(jax.random.key(seed), 4)
    return {
        "bints": noise(splits[0], (O, V, NAUX), (NAUX ** -0.25), 2.5, ((0, 32), (2, 4))),
        "occ_energy": jnp.clip(jax.random.uniform(splits[1], (O,), jnp.float32, -2.0, -0.5), -2.0, -0.5),
        "vir_energy": jnp.clip(jax.random.uniform(splits[2], (V,), jnp.float32, 0.2, 3.0), 0.2, 3.0),
    }


def reference(bints, occ_energy, vir_energy):
    groups = O // OCC_DEV
    blocks = bints.reshape(groups, OCC_DEV, V, NAUX)
    energies = occ_energy.reshape(groups, OCC_DEV)

    def per_group(carry, group):
        block_id = group // N_QUARTER
        quarter_id = group % N_QUARTER
        own = blocks[group].astype(jnp.float32)
        own_energy = energies[group]
        density = jnp.zeros((OCC_DEV, V, NAUX), jnp.float32)
        for step in range(CYCLE):
            partner = (((block_id - step) % N_BLK) * N_QUARTER + quarter_id).astype(jnp.int32)
            other = blocks[partner].astype(jnp.float32)
            other_energy = energies[partner]
            pairint = jnp.einsum("iap,jbp->ijab", own, other)
            denom = (vir_energy[None, None, :, None] + vir_energy[None, None, None, :]
                     - own_energy[:, None, None, None] - other_energy[None, :, None, None])
            amp = pairint / denom
            amp_b = amp.astype(jnp.bfloat16).astype(jnp.float32)
            tilde = (2.0 * amp - jnp.swapaxes(amp, 2, 3)).astype(jnp.bfloat16).astype(jnp.float32)
            density = density + jnp.einsum("ijab,jbp->iap", tilde, other)
            carry = carry + jnp.einsum("ijac,ijbc->ab", amp_b, tilde)
        return carry, density

    total, gammas = lax.scan(per_group, jnp.zeros((V, V), jnp.float32), jnp.arange(groups, dtype=jnp.int32))
    return gammas.reshape(O, V, NAUX), total / PAIRS
```

```python
import functools

import jax
import jax.numpy as jnp
from jax import lax
from jax.experimental import pallas as pl
from jax.experimental.pallas import tpu as pltpu
from jax.sharding import PartitionSpec as P

CYCLE = 3
RING = 4
MESH = pl.DeviceIdType.MESH
NT = (((1,), (1,)), ((), ()))
X, Y, Z = 0, 1, 2


def kernel(
    blocks,
    scale,
    x_ref,
    occ_ref,
    vir_ref,
    gamma_ref,
    vv_ref,
    held,
    raw,
    own_t,
    acc,
    vv,
    amp,
    amp_b,
    tilde,
    vir_col,
    halves,
    half_in,
    by_y,
    by_z,
    by_x,
    local_sem,
    send_sem,
    recv_sem,
    raw_sem,
    out_sem,
    vv_send,
    vv_recv,
):
    piece = x_ref.shape[1]
    b, q = lax.axis_index("blk"), lax.axis_index("quarter")
    col, h, l, k = b // 2, lax.rem(b, 2), q // 2, lax.rem(q, 2)
    cx, cz = col // RING, lax.rem(col, RING)
    near = [q, 2 * l + 1 - k, 2 * (1 - l) + k, 2 * (1 - l) + 1 - k]
    ahead, behind = lax.rem(b + 2, blocks), lax.rem(b + blocks - 2, blocks)
    across = 2 * col + 1 - h

    def along_z(step):
        return 2 * (cx * RING + lax.rem(cz + step, RING)) + h

    def along_x(step):
        return 2 * (lax.rem(cx + step, RING) * RING + cz) + h

    barrier = pltpu.get_barrier_semaphore()
    peers = [(b, near[d]) for d in (1, 2, 3)] + [(across, near[d]) for d in range(4)] + [(ahead, q), (behind, q)]
    peers += [(along_z(s), q) for s in (1, 2, 3)] + [(along_x(s), q) for s in (1, 2, 3)]
    for peer in peers:
        pl.semaphore_signal(barrier, inc=1, device_id=peer, device_id_type=MESH)

    def slot(which, j, p):
        return held.at[which * 2 + j, pl.ds(pl.multiple_of(p * piece, piece), piece), :]

    sends = {0: 0, 1: 0}

    def send(side, src, dst, sem, device):
        n = sends[side]
        copy = pltpu.make_async_remote_copy(
            src_ref=src, dst_ref=dst, send_sem=send_sem.at[n], recv_sem=sem, device_id=device, device_id_type=MESH
        )
        copy.start()
        sends[side] = n + 1

    def to_slot(side, src, which, j, p, device):
        send(side, src, slot(which, j, p), recv_sem.at[which, j, p], device)

    def arrived(dst, sem):
        pltpu.make_async_remote_copy(
            src_ref=dst, dst_ref=dst, send_sem=send_sem.at[0], recv_sem=sem, device_id=(b, near[1]), device_id_type=MESH
        ).wait_recv()

    def slot_arrived(which, j, p):
        arrived(slot(which, j, p), recv_sem.at[which, j, p])

    def mine(r, j):
        return x_ref.at[2 * r + j]

    own_copies = [pltpu.make_async_copy(mine(q, j), slot(X, j, q), local_sem.at[j]) for j in range(2)]
    for copy in own_copies:
        copy.start()
    pl.semaphore_wait(barrier, len(peers))

    @pl.when(h == 0)
    def _():
        for j in range(2):
            for d in (1, 2, 3):
                to_slot(0, mine(near[d], j), X, j, q, (b, near[d]))
            to_slot(0, mine(q, j), Y, j, q, (ahead, q))
            for d in (2, 3):
                to_slot(0, mine(near[d], j), Y, j, q, (across, near[d]))
        for j in range(2):
            for d in (0, 1):
                to_slot(0, mine(near[d], j), Y, j, q, (across, near[d]))

    @pl.when(h == 1)
    def _():
        for j in range(2):
            for d in (1, 2, 3):
                to_slot(1, mine(near[d], j), X, j, q, (b, near[d]))
            to_slot(1, mine(q, j), Z, j, q, (ahead, q))
            for d in (1, 2, 3):
                send(1, mine(near[d], j), raw.at[j, d - 1], raw_sem.at[j, d - 1], (ahead, q))

    acc[...] = jnp.zeros_like(acc)
    vv[...] = jnp.zeros_like(vv)
    vir_col[...] = jnp.transpose(jnp.broadcast_to(vir_ref[...], (128, vir_ref.shape[1])))

    def own_piece(j, d):
        slot_arrived(X, j, near[d])

        @pl.when(h == 0)
        def _():
            to_slot(0, slot(X, j, near[d]), Y, j, near[d], (ahead, q))

    def passed_on(j, d):
        @pl.when(h == 1)
        def _():
            if d == 0:
                slot_arrived(Z, j, q)
                to_slot(1, slot(Z, j, q), Z, j, q, (across, q))
                return
            src = raw.at[j, d - 1]
            arrived(src, raw_sem.at[j, d - 1])
            to_slot(1, src, Z, j, q, (across, near[d]))
            if d == 1 or j == 0:
                to_slot(1, src, Z, j, q, (b, near[d]))

    def second_way():
        @pl.when(h == 1)
        def _():
            for d in (2, 3):
                to_slot(1, slot(X, 1, near[d]), Z, 1, near[d], (ahead, q))

    def last_piece(j):
        @pl.when(h == 0)
        def _():
            slot_arrived(Z, j, q)

        for d in (1, 2, 3):
            slot_arrived(Z, j, near[d])

    def turned(i):
        for n in range(held.shape[1] // 256):
            rows = pl.ds(n * 256, 256)
            own_t[i, :, rows] = jnp.transpose(held[2 * X + i, rows, :])

    def before(t):
        @pl.when(t == 1)
        def _():
            own_piece(1, 2)
            passed_on(0, 2)
            own_piece(1, 3)
            passed_on(0, 3)
            second_way()
            turned(1)

        @pl.when(t == 3)
        def _():
            passed_on(1, 0)

        @pl.when(t == 4)
        def _():
            passed_on(1, 1)
            for p in range(4):
                slot_arrived(Y, 0, p)

        @pl.when(t == 6)
        def _():
            passed_on(1, 2)
            last_piece(0)

        @pl.when(t == 8)
        def _():
            passed_on(1, 3)
            for p in range(4):
                slot_arrived(Y, 1, p)

        @pl.when(t == 10)
        def _():
            last_piece(1)

    for copy in own_copies:
        copy.wait()
    own_piece(0, 1)
    own_piece(1, 1)
    own_piece(0, 2)
    passed_on(0, 0)
    own_piece(0, 3)
    passed_on(0, 1)
    turned(0)

    size = vir_ref.shape[1]

    def pair(t, carry):
        before(t)
        turn, i = t // 2, lax.rem(t, 2)
        which = jnp.where(turn < 2, X, Y + lax.rem(turn, 2))
        j = jnp.where(turn < 2, turn, (turn - 2) // 2)
        back = jnp.where(turn < 2, 0, jnp.where(which == Y, 2 - h, 1 + h))
        partner = lax.rem(b - back + blocks, blocks)
        e_i = occ_ref[(b * 4 + q) * 2 + i]
        e_j = occ_ref[(partner * 4 + q) * 2 + j]
        other = held.at[which * 2 + j]
        for n in range(size // 256):
            cols = pl.ds(n * 256, 256)
            pairint = jnp.dot(own_t[i], other[:, cols], preferred_element_type=jnp.float32)
            for m in range(2):
                lanes = pl.ds(n * 256 + m * 128, 128)
                denom = vir_col[...] + vir_ref[:, lanes] - e_i - e_j
                ratio = pairint[:, m * 128 : (m + 1) * 128] / denom
                amp[:, lanes] = ratio
                amp_b[:, lanes] = ratio.astype(jnp.bfloat16)
        for n in range(size // 128):
            rows = pl.ds(n * 128, 128)
            tilde[rows, :] = (2.0 * amp[rows, :] - jnp.transpose(amp[:, rows])).astype(jnp.bfloat16)
        vv[...] += lax.dot_general(amp_b[...], tilde[...], NT, preferred_element_type=jnp.float32)
        for n in range(held.shape[1] // 256):
            rows = pl.ds(n * 256, 256)
            acc[i, :, rows] += lax.dot_general(tilde[...], other[rows, :], NT, preferred_element_type=jnp.float32)
        return carry

    lax.fori_loop(0, 4 * CYCLE, pair, 0)

    out = pltpu.make_async_copy(acc, gamma_ref, out_sem)
    out.start()

    low = lax.broadcasted_iota(jnp.int32, (8, 256), 0) < 4
    for chip in range(size // 8):
        spot = (chip % RING) * RING * RING + ((chip // RING) % RING) * RING + chip // (RING * RING)
        rows = pl.ds(chip * 8, 8)
        left, right = vv[rows, 0:256], vv[rows, 256:512]
        halves[0, spot] = jnp.where(low, left, pltpu.roll(right, 4, 0))
        halves[1, spot] = jnp.where(low, pltpu.roll(left, 4, 0), right)

    swap = pltpu.make_async_remote_copy(
        src_ref=halves.at[1 - k], dst_ref=half_in, send_sem=vv_send.at[0], recv_sem=vv_recv.at[0],
        device_id=(b, near[1]), device_id_type=MESH,
    )
    swap.start()
    swap.wait()

    def stage(src, landing, first, me, devices):
        copies = [
            pltpu.make_async_remote_copy(
                src_ref=src.at[lax.rem(me + s, RING)], dst_ref=landing.at[s - 1],
                send_sem=vv_send.at[first + s - 1], recv_sem=vv_recv.at[first + s - 1],
                device_id=devices[s - 1], device_id_type=MESH,
            )
            for s in (1, 2, 3)
        ]
        for copy in copies:
            copy.start()
        for copy in copies:
            copy.wait()
        return src[me] + landing[0] + landing[1] + landing[2]

    here = 2 * h + l
    column = []
    for s in (1, 2, 3):
        there = lax.rem(here + s, RING)
        column.append((2 * col + there // 2, 2 * lax.rem(there, 2) + k))
    half_in[...] += halves[k]
    by_chip = half_in.reshape(RING, RING * RING, 8, 256)
    by_z_src = stage(by_chip, by_y, 1, here, column)
    halves[0, 0:16] = by_z_src
    by_row = halves.at[0, pl.ds(0, 16)].reshape(RING, RING, 8, 256)
    by_x_src = stage(by_row, by_z, 4, cz, [(along_z(s), q) for s in (1, 2, 3)])
    halves[1, 0:4] = by_x_src
    total = stage(halves.at[1, pl.ds(0, 4)], by_x, 7, cx, [(along_x(s), q) for s in (1, 2, 3)]) * scale
    vv_ref[:, 0:256] = total[0:4]
    vv_ref[:, 256:512] = total[4:8]

    for side in (0, 1):

        @pl.when(h == side)
        def _():
            for n in range(sends[side]):
                pltpu.make_async_remote_copy(
                    src_ref=x_ref.at[0], dst_ref=raw.at[0, 0], send_sem=send_sem.at[n], recv_sem=recv_sem.at[0, 0, 0],
                    device_id=(b, near[1]), device_id_type=MESH,
                ).wait_send()

    out.wait()


def per_device(blocks, quarters, bints, occ_energy, vir_energy):
    rows, size, piece = bints.shape
    naux = piece * quarters
    pair_rows = rows // quarters
    f32, bf16 = jnp.float32, jnp.bfloat16
    scale = 1.0 / float(pair_rows * blocks * quarters * CYCLE * pair_rows)
    dma = pltpu.SemaphoreType.DMA
    chips = size // 8
    return pl.pallas_call(
        functools.partial(kernel, blocks, scale),
        out_shape=(
            jax.ShapeDtypeStruct((pair_rows, size, naux), f32),
            jax.ShapeDtypeStruct((size // (blocks * quarters), size), f32),
        ),
        in_specs=[
            pl.BlockSpec(memory_space=pl.ANY),
            pl.BlockSpec(memory_space=pltpu.SMEM),
            pl.BlockSpec(memory_space=pltpu.VMEM),
        ],
        out_specs=(pl.BlockSpec(memory_space=pl.ANY), pl.BlockSpec(memory_space=pltpu.VMEM)),
        scratch_shapes=[
            pltpu.VMEM((3 * pair_rows, naux, size), bf16),
            pltpu.VMEM((pair_rows, 3, piece, size), bf16),
            pltpu.VMEM((pair_rows, size, naux), bf16),
            pltpu.VMEM((pair_rows, size, naux), f32),
            pltpu.VMEM((size, size), f32),
            pltpu.VMEM((size, size), f32),
            pltpu.VMEM((size, size), bf16),
            pltpu.VMEM((size, size), bf16),
            pltpu.VMEM((size, 128), f32),
            pltpu.VMEM((2, chips, 8, 256), f32),
            pltpu.VMEM((chips, 8, 256), f32),
            pltpu.VMEM((3, 16, 8, 256), f32),
            pltpu.VMEM((3, 4, 8, 256), f32),
            pltpu.VMEM((3, 8, 256), f32),
            dma((2,)),
            dma((40,)),
            dma((3, 2, 4)),
            dma((2, 3)),
            dma,
            dma((10,)),
            dma((10,)),
        ],
        compiler_params=pltpu.CompilerParams(
            collective_id=0, has_side_effects=True, vmem_limit_bytes=60 * 2**20
        ),
        name="pair_densities",
    )(jnp.swapaxes(bints, 1, 2), occ_energy, vir_energy.reshape(1, size))


def solution(mesh):
    return jax.shard_map(
        functools.partial(per_device, mesh.shape["blk"], mesh.shape["quarter"]),
        mesh=mesh,
        in_specs=(P("blk", None, "quarter"), P(), P()),
        out_specs=(P(("blk", "quarter"), None, None), P(("blk", "quarter"), None)),
        check_vma=False,
    )
```

```python
import functools

import jax
import jax.numpy as jnp
from jax import lax
from jax.experimental import pallas as pl
from jax.experimental.pallas import tpu as pltpu
from jax.sharding import PartitionSpec as P

CYCLE = 3
RING = 4
MESH = pl.DeviceIdType.MESH
NT = (((1,), (1,)), ((), ()))
X, Y, Z = 0, 1, 2


def kernel(
    blocks,
    scale,
    x_ref,
    occ_ref,
    vir_ref,
    acc,
    vv_ref,
    held,
    raw,
    relay,
    own_t,
    vv,
    amp,
    amp_b,
    tilde,
    vir_col,
    halves,
    half_in,
    first_in,
    second,
    second_in,
    third,
    third_in,
    local_sem,
    send_sem,
    recv_sem,
    raw_sem,
    relay_sem,
    vv_send,
    vv_recv,
):
    piece = x_ref.shape[1]
    b, q = lax.axis_index("blk"), lax.axis_index("quarter")
    col, h, l, k = b // 2, lax.rem(b, 2), q // 2, lax.rem(q, 2)
    cx, cz = col // RING, lax.rem(col, RING)
    near = [q, 2 * l + 1 - k, 2 * (1 - l) + k, 2 * (1 - l) + 1 - k]
    ahead, behind = lax.rem(b + 2, blocks), lax.rem(b + blocks - 2, blocks)
    across = 2 * col + 1 - h

    def along_z(step):
        return 2 * (cx * RING + lax.rem(cz + step, RING)) + h

    def along_x(step):
        return 2 * (lax.rem(cx + step, RING) * RING + cz) + h

    barrier = pltpu.get_barrier_semaphore()
    peers = [(b, near[d]) for d in (1, 2, 3)] + [(across, near[d]) for d in range(4)] + [(ahead, q), (behind, q)]
    peers += [(along_z(s), q) for s in (1, 2, 3)] + [(along_x(s), q) for s in (1, 2, 3)]
    for peer in peers:
        pl.semaphore_signal(barrier, inc=1, device_id=peer, device_id_type=MESH)

    def slot(which, j, p):
        return held.at[which * 2 + j, pl.ds(pl.multiple_of(p * piece, piece), piece), :]

    sends = {0: 0, 1: 0}

    def send(side, src, dst, sem, device):
        n = sends[side]
        copy = pltpu.make_async_remote_copy(
            src_ref=src, dst_ref=dst, send_sem=send_sem.at[n], recv_sem=sem, device_id=device, device_id_type=MESH
        )
        copy.start()
        sends[side] = n + 1

    def to_slot(side, src, which, j, p, device):
        send(side, src, slot(which, j, p), recv_sem.at[which, j, p], device)

    def arrived(dst, sem):
        pltpu.make_async_remote_copy(
            src_ref=dst, dst_ref=dst, send_sem=send_sem.at[0], recv_sem=sem, device_id=(b, near[1]), device_id_type=MESH
        ).wait_recv()

    def slot_arrived(which, j, p):
        arrived(slot(which, j, p), recv_sem.at[which, j, p])

    def mine(r, j):
        return x_ref.at[2 * r + j]

    own_copies = [pltpu.make_async_copy(mine(q, j), slot(X, j, q), local_sem.at[j]) for j in range(2)]
    for copy in own_copies:
        copy.start()
    pl.semaphore_wait(barrier, len(peers))

    @pl.when(h == 0)
    def _():
        for d in (1, 2, 3):
            to_slot(0, mine(near[d], 0), X, 0, q, (b, near[d]))
        to_slot(0, mine(near[1], 1), X, 1, q, (b, near[1]))
        to_slot(0, mine(q, 0), Y, 0, q, (ahead, q))
        for d in (2, 3):
            to_slot(0, mine(near[d], 0), Y, 0, q, (across, near[d]))
        for d in (2, 3):
            to_slot(0, mine(near[d], 1), X, 1, q, (b, near[d]))
        to_slot(0, mine(q, 1), Y, 1, q, (ahead, q))
        for d in (2, 3):
            to_slot(0, mine(near[d], 1), Y, 1, q, (across, near[d]))
        for j in range(2):
            for d in (0, 1):
                to_slot(0, mine(near[d], j), Y, j, q, (across, near[d]))

    @pl.when(h == 1)
    def _():
        send(1, mine(near[3], 1), relay.at[0], relay_sem.at[0], (across, near[3]))
        for d in (1, 2, 3):
            to_slot(1, mine(near[d], 0), X, 0, q, (b, near[d]))
        to_slot(1, mine(near[1], 1), X, 1, q, (b, near[1]))
        for j in range(2):
            to_slot(1, mine(q, j), Z, j, q, (ahead, q))
            for d in (1, 2, 3)[: 3 - j]:
                send(1, mine(near[d], j), raw.at[j, d - 1], raw_sem.at[j, d - 1], (ahead, q))

    acc[...] = jnp.zeros_like(acc)
    vv[...] = jnp.zeros_like(vv)
    vir_col[...] = jnp.transpose(jnp.broadcast_to(vir_ref[...], (128, vir_ref.shape[1])))

    def own_piece(j, d):
        slot_arrived(X, j, near[d])

        @pl.when(h == 0)
        def _():
            to_slot(0, slot(X, j, near[d]), Y, j, near[d], (ahead, q))

    def passed_on(j, d):
        @pl.when(h == 1)
        def _():
            if d == 0:
                slot_arrived(Z, j, q)
                if j == 1:
                    send(1, slot(Z, j, q), relay.at[1], relay_sem.at[1], (across, near[2]))
                    return
                to_slot(1, slot(Z, j, q), Z, j, q, (across, q))
                for own in (2, 3):
                    to_slot(1, mine(near[own], 1), X, 1, q, (b, near[own]))
                return
            src = raw.at[j, d - 1]
            arrived(src, raw_sem.at[j, d - 1])
            to_slot(1, src, Z, j, q, (across, near[d]))
            if d == 1 or j == 0:
                to_slot(1, src, Z, j, q, (b, near[d]))

    def second_way():
        @pl.when(h == 1)
        def _():
            for d in (2, 3):
                to_slot(1, slot(X, 1, near[d]), Z, 1, near[d], (ahead, q))

    def relayed(n):
        @pl.when(h == 0)
        def _():
            arrived(relay.at[n], relay_sem.at[n])
            if n == 0:
                to_slot(0, relay.at[n], Z, 1, near[3], (ahead, q))
            else:
                to_slot(0, relay.at[n], Z, 1, near[2], (b, near[2]))

    def last_piece(j):
        @pl.when(h == 0)
        def _():
            slot_arrived(Z, j, q)

        for d in (1, 2, 3):
            slot_arrived(Z, j, near[d])

    def turned(i):
        for n in range(held.shape[1] // 256):
            rows = pl.ds(n * 256, 256)
            own_t[i, :, rows] = jnp.transpose(held[2 * X + i, rows, :])

    def before(t):
        @pl.when(t == 1)
        def _():
            passed_on(0, 2)
            own_piece(1, 2)
            passed_on(0, 3)
            own_piece(1, 3)
            second_way()
            relayed(0)
            passed_on(1, 0)
            turned(1)

        @pl.when(t == 4)
        def _():
            passed_on(1, 1)
            relayed(1)
            for p in range(4):
                slot_arrived(Y, 0, p)

        @pl.when(t == 6)
        def _():
            passed_on(1, 2)
            last_piece(0)

        @pl.when(t == 8)
        def _():
            for p in range(4):
                slot_arrived(Y, 1, p)

        @pl.when(t == 10)
        def _():
            last_piece(1)

    for copy in own_copies:
        copy.wait()
    own_piece(0, 1)
    own_piece(1, 1)
    own_piece(0, 2)
    passed_on(0, 0)
    own_piece(0, 3)
    passed_on(0, 1)
    turned(0)

    size = vir_ref.shape[1]

    pairs = 4 * CYCLE

    def place(t):
        turn = t // 2
        which = jnp.where(turn < 2, X, Y + lax.rem(turn, 2))
        j = jnp.where(turn < 2, turn, (turn - 2) // 2)
        return lax.rem(t, 2), which, j

    def to_gamma(t):
        i, which, j = place(t)
        other = held.at[which * 2 + j]
        for n in range(held.shape[1] // 256):
            rows = pl.ds(n * 256, 256)
            acc[i, :, rows] += lax.dot_general(tilde[i], other[rows, :], NT, preferred_element_type=jnp.float32)

    def pair(t, carry):
        before(t)
        i, which, j = place(t)
        back = jnp.where(which == X, 0, jnp.where(which == Y, 2 - h, 1 + h))
        partner = lax.rem(b - back + blocks, blocks)
        e_i = occ_ref[(b * 4 + q) * 2 + i]
        e_j = occ_ref[(partner * 4 + q) * 2 + j]
        other = held.at[which * 2 + j]
        for n in range(size // 256):
            cols = pl.ds(n * 256, 256)
            pairint = jnp.dot(own_t[i], other[:, cols], preferred_element_type=jnp.float32)
            for m in range(2):
                lanes = pl.ds(n * 256 + m * 128, 128)
                denom = vir_col[...] + vir_ref[:, lanes] - e_i - e_j
                ratio = pairint[:, m * 128 : (m + 1) * 128] / denom
                amp[:, lanes] = ratio
                amp_b[:, lanes] = ratio.astype(jnp.bfloat16)
        for n in range(size // 128):
            rows = pl.ds(n * 128, 128)
            tilde[i, rows, :] = (2.0 * amp[rows, :] - jnp.transpose(amp[:, rows])).astype(jnp.bfloat16)
        vv[...] += lax.dot_general(amp_b[...], tilde[i], NT, preferred_element_type=jnp.float32)

        @pl.when(t < pairs - 2)
        def _():
            to_gamma(t)

        return carry

    lax.fori_loop(0, pairs, pair, 0)

    low = lax.broadcasted_iota(jnp.int32, (8, 256), 0) < 4
    square = RING * RING
    for chip in range(size // 8):
        spot = (chip % RING) * square + ((chip // RING) % RING) * RING + chip // square
        rows = pl.ds(chip * 8, 8)
        left, right = vv[rows, 0:256], vv[rows, 256:512]
        for core, block in enumerate((jnp.where(low, left, pltpu.roll(right, 4, 0)), jnp.where(low, pltpu.roll(left, 4, 0), right))):
            halves[core, 0, spot] = block[:, 0:128]
            halves[core, 1, chip] = block[:, 128:256]

    swap = pltpu.make_async_remote_copy(
        src_ref=halves.at[1 - k], dst_ref=half_in, send_sem=vv_send.at[0], recv_sem=vv_recv.at[0],
        device_id=(b, near[1]), device_id_type=MESH,
    )
    swap.start()
    to_gamma(pairs - 2)
    to_gamma(pairs - 1)
    swap.wait()
    half_in[...] += halves[k]

    here = 2 * h + l
    column = []
    for s in (1, 2, 3):
        there = lax.rem(here + s, RING)
        column.append((2 * col + there // 2, 2 * lax.rem(there, 2) + k))
    rings = {
        "y": (here, column),
        "z": (cz, [(along_z(s), q) for s in (1, 2, 3)]),
        "x": (cx, [(along_x(s), q) for s in (1, 2, 3)]),
    }

    def stage(src, landing, first, axis):
        me, devices = rings[axis]
        copies = [
            pltpu.make_async_remote_copy(
                src_ref=src.at[lax.rem(me + s, RING)], dst_ref=landing.at[s - 1],
                send_sem=vv_send.at[first + s - 1], recv_sem=vv_recv.at[first + s - 1],
                device_id=devices[s - 1], device_id_type=MESH,
            )
            for s in (1, 2, 3)
        ]
        for copy in copies:
            copy.start()

        def total():
            for copy in copies:
                copy.wait()
            return src[me] + landing[0] + landing[1] + landing[2]

        return total

    orders = ("yzx", "xzy")
    waits = [stage(half_in.at[n].reshape(RING, square, 8, 128), first_in.at[n], 1 + 3 * n, orders[n][0]) for n in range(2)]
    for n in range(2):
        second[n] = waits[n]()
        waits[n] = stage(second.at[n].reshape(RING, RING, 8, 128), second_in.at[n], 7 + 3 * n, orders[n][1])
    for n in range(2):
        third[n] = waits[n]()
        waits[n] = stage(third.at[n], third_in.at[n], 13 + 3 * n, orders[n][2])
    for n in range(2):
        total = waits[n]() * scale
        lanes = pl.ds(n * 128, 128)
        vv_ref[:, lanes] = total[0:4]
        vv_ref[:, pl.ds(256 + n * 128, 128)] = total[4:8]

    for side in (0, 1):

        @pl.when(h == side)
        def _():
            for n in range(sends[side]):
                pltpu.make_async_remote_copy(
                    src_ref=x_ref.at[0], dst_ref=raw.at[0, 0], send_sem=send_sem.at[n], recv_sem=recv_sem.at[0, 0, 0],
                    device_id=(b, near[1]), device_id_type=MESH,
                ).wait_send()


def per_device(blocks, quarters, bints, occ_energy, vir_energy):
    rows, size, piece = bints.shape
    naux = piece * quarters
    pair_rows = rows // quarters
    f32, bf16 = jnp.float32, jnp.bfloat16
    scale = 1.0 / float(pair_rows * blocks * quarters * CYCLE * pair_rows)
    dma = pltpu.SemaphoreType.DMA
    chips = size // 8
    return pl.pallas_call(
        functools.partial(kernel, blocks, scale),
        out_shape=(
            jax.ShapeDtypeStruct((pair_rows, size, naux), f32),
            jax.ShapeDtypeStruct((size // (blocks * quarters), size), f32),
        ),
        in_specs=[
            pl.BlockSpec(memory_space=pltpu.HBM),
            pl.BlockSpec(memory_space=pltpu.SMEM),
            pl.BlockSpec(memory_space=pltpu.VMEM),
        ],
        out_specs=(pl.BlockSpec(memory_space=pltpu.VMEM), pl.BlockSpec(memory_space=pltpu.VMEM)),
        scratch_shapes=[
            pltpu.VMEM((3 * pair_rows, naux, size), bf16),
            pltpu.VMEM((pair_rows, 3, piece, size), bf16),
            pltpu.VMEM((2, piece, size), bf16),
            pltpu.VMEM((pair_rows, size, naux), bf16),
            pltpu.VMEM((size, size), f32),
            pltpu.VMEM((size, size), f32),
            pltpu.VMEM((size, size), bf16),
            pltpu.VMEM((pair_rows, size, size), bf16),
            pltpu.VMEM((size, 128), f32),
            pltpu.VMEM((2, 2, chips, 8, 128), f32),
            pltpu.VMEM((2, chips, 8, 128), f32),
            pltpu.VMEM((2, 3, 16, 8, 128), f32),
            pltpu.VMEM((2, 16, 8, 128), f32),
            pltpu.VMEM((2, 3, 4, 8, 128), f32),
            pltpu.VMEM((2, 4, 8, 128), f32),
            pltpu.VMEM((2, 3, 8, 128), f32),
            dma((2,)),
            dma((40,)),
            dma((3, 2, 4)),
            dma((2, 3)),
            dma((2,)),
            dma((19,)),
            dma((19,)),
        ],
        compiler_params=pltpu.CompilerParams(
            collective_id=0, has_side_effects=True, vmem_limit_bytes=40 * 2**20
        ),
        name="pair_densities",
    )(jnp.swapaxes(bints, 1, 2), occ_energy, vir_energy.reshape(1, size))


def solution(mesh):
    return jax.shard_map(
        functools.partial(per_device, mesh.shape["blk"], mesh.shape["quarter"]),
        mesh=mesh,
        in_specs=(P("blk", None, "quarter"), P(), P()),
        out_specs=(P(("blk", "quarter"), None, None), P(("blk", "quarter"), None)),
        check_vma=False,
    )
```

```python
import functools

import jax
import jax.numpy as jnp
from jax import lax
from jax.experimental import pallas as pl
from jax.experimental.pallas import tpu as pltpu
from jax.sharding import PartitionSpec as P

CYCLE = 3
RING = 4
MESH = pl.DeviceIdType.MESH
NT = (((1,), (1,)), ((), ()))
X, Y, Z = 0, 1, 2


def kernel(
    blocks,
    scale,
    x_ref,
    occ_ref,
    vir_ref,
    acc,
    vv_ref,
    held,
    raw,
    relay,
    back,
    own_t,
    vv,
    amp,
    amp_b,
    tilde,
    vir_col,
    halves,
    half_in,
    first_in,
    second,
    second_in,
    third,
    third_in,
    local_sem,
    send_sem,
    recv_sem,
    raw_sem,
    relay_sem,
    back_send,
    back_recv,
    vv_send,
    vv_recv,
):
    piece = x_ref.shape[1]
    b, q = lax.axis_index("blk"), lax.axis_index("quarter")
    col, h, l, k = b // 2, lax.rem(b, 2), q // 2, lax.rem(q, 2)
    cx, cz = col // RING, lax.rem(col, RING)
    near = [q, 2 * l + 1 - k, 2 * (1 - l) + k, 2 * (1 - l) + 1 - k]
    ahead, behind = lax.rem(b + 2, blocks), lax.rem(b + blocks - 2, blocks)
    across = 2 * col + 1 - h

    def along_z(step):
        return 2 * (cx * RING + lax.rem(cz + step, RING)) + h

    def along_x(step):
        return 2 * (lax.rem(cx + step, RING) * RING + cz) + h

    barrier = pltpu.get_barrier_semaphore()
    peers = [(b, near[d]) for d in (1, 2, 3)] + [(across, near[d]) for d in range(4)] + [(ahead, q), (behind, q)]
    peers += [(along_z(s), q) for s in (1, 2, 3)] + [(along_x(s), q) for s in (1, 2, 3)]
    for peer in peers:
        pl.semaphore_signal(barrier, inc=1, device_id=peer, device_id_type=MESH)

    def slot(which, j, p):
        return held.at[which * 2 + j, pl.ds(pl.multiple_of(p * piece, piece), piece), :]

    sends = {0: 0, 1: 0}

    def send(side, src, dst, sem, device):
        n = sends[side]
        copy = pltpu.make_async_remote_copy(
            src_ref=src, dst_ref=dst, send_sem=send_sem.at[n], recv_sem=sem, device_id=device, device_id_type=MESH
        )
        copy.start()
        sends[side] = n + 1

    def to_slot(side, src, which, j, p, device):
        send(side, src, slot(which, j, p), recv_sem.at[which, j, p], device)

    def arrived(dst, sem):
        pltpu.make_async_remote_copy(
            src_ref=dst, dst_ref=dst, send_sem=send_sem.at[0], recv_sem=sem, device_id=(b, near[1]), device_id_type=MESH
        ).wait_recv()

    def slot_arrived(which, j, p):
        arrived(slot(which, j, p), recv_sem.at[which, j, p])

    def mine(r, j):
        return x_ref.at[2 * r + j]

    own_copies = [pltpu.make_async_copy(mine(q, j), slot(X, j, q), local_sem.at[j]) for j in range(2)]
    for copy in own_copies:
        copy.start()
    pl.semaphore_wait(barrier, len(peers))

    odd = lax.rem(cz, 2)
    halfway = jnp.where(odd == 1, along_z(2), along_z(3))

    def send_back(side, src, n):
        send(side, src, back.at[odd, n], back_recv.at[odd, n], (halfway, q))

    @pl.when(h == 0)
    def _():
        for d in (1, 2, 3):
            to_slot(0, mine(near[d], 0), X, 0, q, (b, near[d]))
        to_slot(0, mine(near[1], 1), X, 1, q, (b, near[1]))
        to_slot(0, mine(q, 0), Y, 0, q, (ahead, q))
        send_back(0, mine(q, 1), 0)
        for d in (2, 3):
            to_slot(0, mine(near[d], 0), Y, 0, q, (across, near[d]))
        for d in (2, 3):
            to_slot(0, mine(near[d], 1), X, 1, q, (b, near[d]))
        for d in (2, 3):
            to_slot(0, mine(near[d], 1), Y, 1, q, (across, near[d]))
        for j in range(2):
            for d in (0, 1):
                to_slot(0, mine(near[d], j), Y, j, q, (across, near[d]))

    @pl.when(h == 1)
    def _():
        for d in (2, 3):
            send(1, mine(near[d], 1), relay.at[d - 2], relay_sem.at[d - 2], (across, near[d]))
        for d in (1, 2, 3):
            to_slot(1, mine(near[d], 0), X, 0, q, (b, near[d]))
        to_slot(1, mine(near[1], 1), X, 1, q, (b, near[1]))
        to_slot(1, mine(q, 0), Z, 0, q, (ahead, q))
        send_back(1, mine(near[1], 0), 0)
        for d in (2, 3):
            send(1, mine(near[d], 0), raw.at[0, d - 1], raw_sem.at[0, d - 1], (ahead, q))
        to_slot(1, mine(q, 1), Z, 1, q, (ahead, q))
        send_back(1, mine(near[1], 1), 1)

    acc[...] = jnp.zeros_like(acc)
    vv[...] = jnp.zeros_like(vv)
    vir_col[...] = jnp.transpose(jnp.broadcast_to(vir_ref[...], (128, vir_ref.shape[1])))

    def own_piece(j, d):
        slot_arrived(X, j, near[d])

        @pl.when(h == 0)
        def _():
            if (j, d) == (1, 1):
                send_back(0, slot(X, j, near[d]), 1)
            else:
                to_slot(0, slot(X, j, near[d]), Y, j, near[d], (ahead, q))

        if d > 1:

            @pl.when(h == 1)
            def _():
                to_slot(1, slot(X, j, near[d]), Z, j, near[d], (ahead, q))

    def passed_on(j, d):
        @pl.when(h == 1)
        def _():
            if d == 0:
                slot_arrived(Z, j, q)
                to_slot(1, slot(Z, j, q), Z, j, q, (across, q))
                if j == 0:
                    for own in (2, 3):
                        to_slot(1, mine(near[own], 1), X, 1, q, (b, near[own]))
                return
            src = raw.at[j, d - 1]
            arrived(src, raw_sem.at[j, d - 1])
            to_slot(1, src, Z, j, q, (across, near[d]))
            if d == 1:
                to_slot(1, src, Z, j, q, (b, near[d]))

    def relayed():
        @pl.when(h == 0)
        def _():
            for d in (2, 3):
                arrived(relay.at[d - 2], relay_sem.at[d - 2])
                to_slot(0, relay.at[d - 2], Z, 1, near[d], (ahead, q))

    def handed_back(n, act):
        for e in (0, 1):
            source = cx * RING + lax.rem(cz + 1 + e, RING)
            device = (lax.rem(2 * source + 2 + h, blocks), q)
            copy = functools.partial(
                pltpu.make_async_remote_copy,
                src_ref=back.at[e, n], send_sem=back_send.at[e, n], device_id=device, device_id_type=MESH,
            )
            to_raw = copy(dst_ref=raw.at[n, 0], recv_sem=raw_sem.at[n, 0])
            if act == "wait":

                @pl.when(odd == 1)
                def _():
                    to_raw.wait_send()

                continue

            @pl.when(odd == 1)
            def _():
                arrived(back.at[e, n], back_recv.at[e, n])

            @pl.when(jnp.logical_and(odd == 1, h == 1))
            def _():
                to_raw.start()

            p = near[n]

            @pl.when(jnp.logical_and(odd == 1, h == 0))
            def _():
                copy(dst_ref=slot(Y, 1, p), recv_sem=recv_sem.at[Y, 1, p]).start()

    def last_piece(j):
        @pl.when(h == 0)
        def _():
            slot_arrived(Z, j, q)

        for d in (1, 2, 3):
            slot_arrived(Z, j, near[d])

    def turned(i):
        for n in range(held.shape[1] // 256):
            rows = pl.ds(n * 256, 256)
            own_t[i, :, rows] = jnp.transpose(held[2 * X + i, rows, :])

    def before(t):
        @pl.when(t == 1)
        def _():
            passed_on(0, 3)
            handed_back(0, "start")
            own_piece(1, 2)
            passed_on(1, 0)
            own_piece(1, 3)
            relayed()
            turned(1)

        @pl.when(t == 2)
        def _():
            handed_back(1, "start")

        @pl.when(t == 3)
        def _():
            passed_on(0, 1)

        @pl.when(t == 4)
        def _():
            for p in range(4):
                slot_arrived(Y, 0, p)

        @pl.when(t == 6)
        def _():
            passed_on(1, 1)
            last_piece(0)

        @pl.when(t == 8)
        def _():
            for p in range(4):
                slot_arrived(Y, 1, p)

        @pl.when(t == 10)
        def _():
            last_piece(1)

    for copy in own_copies:
        copy.wait()
    own_piece(0, 1)
    own_piece(1, 1)
    own_piece(0, 2)
    passed_on(0, 0)
    own_piece(0, 3)
    passed_on(0, 2)
    turned(0)

    size = vir_ref.shape[1]

    pairs, late = 4 * CYCLE, tilde.shape[0]

    def place(t):
        turn = t // 2
        which = jnp.where(turn < 2, X, Y + lax.rem(turn, 2))
        j = jnp.where(turn < 2, turn, (turn - 2) // 2)
        return lax.rem(t, 2), which, j

    def to_gamma(t):
        i, which, j = place(t)
        other = held.at[which * 2 + j]
        for n in range(held.shape[1] // 256):
            rows = pl.ds(n * 256, 256)
            acc[i, :, rows] += lax.dot_general(tilde[lax.rem(t, late)], other[rows, :], NT, preferred_element_type=jnp.float32)

    def pair(t, carry):
        before(t)
        i, which, j = place(t)
        behind_by = jnp.where(which == X, 0, jnp.where(which == Y, 2 - h, 1 + h))
        partner = lax.rem(b - behind_by + blocks, blocks)
        e_i = occ_ref[(b * 4 + q) * 2 + i]
        e_j = occ_ref[(partner * 4 + q) * 2 + j]
        other = held.at[which * 2 + j]
        for n in range(size // 256):
            cols = pl.ds(n * 256, 256)
            pairint = jnp.dot(own_t[i], other[:, cols], preferred_element_type=jnp.float32)
            for m in range(2):
                lanes = pl.ds(n * 256 + m * 128, 128)
                denom = vir_col[...] + vir_ref[:, lanes] - e_i - e_j
                ratio = pairint[:, m * 128 : (m + 1) * 128] / denom
                amp[:, lanes] = ratio
                amp_b[:, lanes] = ratio.astype(jnp.bfloat16)
        for n in range(size // 128):
            rows = pl.ds(n * 128, 128)
            tilde[lax.rem(t, late), rows, :] = (2.0 * amp[rows, :] - jnp.transpose(amp[:, rows])).astype(jnp.bfloat16)
        vv[...] += lax.dot_general(amp_b[...], tilde[lax.rem(t, late)], NT, preferred_element_type=jnp.float32)

        @pl.when(t < pairs - late)
        def _():
            to_gamma(t)

        return carry

    lax.fori_loop(0, pairs, pair, 0)

    low = lax.broadcasted_iota(jnp.int32, (8, 256), 0) < 4
    square = RING * RING
    for chip in range(size // 8):
        spot = (chip % RING) * square + ((chip // RING) % RING) * RING + chip // square
        rows = pl.ds(chip * 8, 8)
        left, right = vv[rows, 0:256], vv[rows, 256:512]
        for core, block in enumerate((jnp.where(low, left, pltpu.roll(right, 4, 0)), jnp.where(low, pltpu.roll(left, 4, 0), right))):
            halves[core, 0, spot] = block[:, 0:128]
            halves[core, 1, chip] = block[:, 128:256]

    swap = pltpu.make_async_remote_copy(
        src_ref=halves.at[1 - k], dst_ref=half_in, send_sem=vv_send.at[0], recv_sem=vv_recv.at[0],
        device_id=(b, near[1]), device_id_type=MESH,
    )
    swap.start()
    to_gamma(pairs - 4)
    to_gamma(pairs - 3)
    swap.wait()
    half_in[...] += halves[k]

    here = 2 * h + l
    column = []
    for s in (1, 2, 3):
        there = lax.rem(here + s, RING)
        column.append((2 * col + there // 2, 2 * lax.rem(there, 2) + k))
    rings = {
        "y": (here, column),
        "z": (cz, [(along_z(s), q) for s in (1, 2, 3)]),
        "x": (cx, [(along_x(s), q) for s in (1, 2, 3)]),
    }

    def stage(src, landing, first, axis):
        me, devices = rings[axis]
        copies = [
            pltpu.make_async_remote_copy(
                src_ref=src.at[lax.rem(me + s, RING)], dst_ref=landing.at[s - 1],
                send_sem=vv_send.at[first + s - 1], recv_sem=vv_recv.at[first + s - 1],
                device_id=devices[s - 1], device_id_type=MESH,
            )
            for s in (1, 2, 3)
        ]
        for copy in copies:
            copy.start()

        def total():
            for copy in copies:
                copy.wait()
            return src[me] + landing[0] + landing[1] + landing[2]

        return total

    orders = ("yzx", "xzy")
    waits = [stage(half_in.at[n].reshape(RING, square, 8, 128), first_in.at[n], 1 + 3 * n, orders[n][0]) for n in range(2)]
    to_gamma(pairs - 2)
    to_gamma(pairs - 1)
    for n in range(2):
        second[n] = waits[n]()
        waits[n] = stage(second.at[n].reshape(RING, RING, 8, 128), second_in.at[n], 7 + 3 * n, orders[n][1])
    for n in range(2):
        third[n] = waits[n]()
        waits[n] = stage(third.at[n], third_in.at[n], 13 + 3 * n, orders[n][2])
    for n in range(2):
        total = waits[n]() * scale
        lanes = pl.ds(n * 128, 128)
        vv_ref[:, lanes] = total[0:4]
        vv_ref[:, pl.ds(256 + n * 128, 128)] = total[4:8]

    for n in range(2):
        handed_back(n, "wait")
    for side in (0, 1):

        @pl.when(h == side)
        def _():
            for n in range(sends[side]):
                pltpu.make_async_remote_copy(
                    src_ref=x_ref.at[0], dst_ref=raw.at[0, 0], send_sem=send_sem.at[n], recv_sem=recv_sem.at[0, 0, 0],
                    device_id=(b, near[1]), device_id_type=MESH,
                ).wait_send()


def per_device(blocks, quarters, bints, occ_energy, vir_energy):
    rows, size, piece = bints.shape
    naux = piece * quarters
    pair_rows = rows // quarters
    f32, bf16 = jnp.float32, jnp.bfloat16
    scale = 1.0 / float(pair_rows * blocks * quarters * CYCLE * pair_rows)
    dma = pltpu.SemaphoreType.DMA
    chips = size // 8
    return pl.pallas_call(
        functools.partial(kernel, blocks, scale),
        out_shape=(
            jax.ShapeDtypeStruct((pair_rows, size, naux), f32),
            jax.ShapeDtypeStruct((size // (blocks * quarters), size), f32),
        ),
        in_specs=[
            pl.BlockSpec(memory_space=pltpu.HBM),
            pl.BlockSpec(memory_space=pltpu.SMEM),
            pl.BlockSpec(memory_space=pltpu.VMEM),
        ],
        out_specs=(pl.BlockSpec(memory_space=pltpu.VMEM), pl.BlockSpec(memory_space=pltpu.VMEM)),
        scratch_shapes=[
            pltpu.VMEM((3 * pair_rows, naux, size), bf16),
            pltpu.VMEM((pair_rows, 3, piece, size), bf16),
            pltpu.VMEM((2, piece, size), bf16),
            pltpu.VMEM((2, 2, piece, size), bf16),
            pltpu.VMEM((pair_rows, size, naux), bf16),
            pltpu.VMEM((size, size), f32),
            pltpu.VMEM((size, size), f32),
            pltpu.VMEM((size, size), bf16),
            pltpu.VMEM((4, size, size), bf16),
            pltpu.VMEM((size, 128), f32),
            pltpu.VMEM((2, 2, chips, 8, 128), f32),
            pltpu.VMEM((2, chips, 8, 128), f32),
            pltpu.VMEM((2, 3, 16, 8, 128), f32),
            pltpu.VMEM((2, 16, 8, 128), f32),
            pltpu.VMEM((2, 3, 4, 8, 128), f32),
            pltpu.VMEM((2, 4, 8, 128), f32),
            pltpu.VMEM((2, 3, 8, 128), f32),
            dma((2,)),
            dma((40,)),
            dma((3, 2, 4)),
            dma((2, 3)),
            dma((2,)),
            dma((2, 2)),
            dma((2, 2)),
            dma((19,)),
            dma((19,)),
        ],
        compiler_params=pltpu.CompilerParams(
            collective_id=0, has_side_effects=True, vmem_limit_bytes=40 * 2**20
        ),
        name="pair_densities",
    )(pltpu.with_memory_space_constraint(jnp.swapaxes(bints, 1, 2), pltpu.HBM), pltpu.with_memory_space_constraint(occ_energy, pltpu.HBM), pltpu.with_memory_space_constraint(vir_energy.reshape(1, size), pltpu.HBM))


def solution(mesh):
    return jax.shard_map(
        functools.partial(per_device, mesh.shape["blk"], mesh.shape["quarter"]),
        mesh=mesh,
        in_specs=(P("blk", None, "quarter"), P(), P()),
        out_specs=(P(("blk", "quarter"), None, None), P(("blk", "quarter"), None)),
        check_vma=False,
    )
```

```python
import functools

import jax
import jax.numpy as jnp
from jax import lax
from jax.experimental import pallas as pl
from jax.experimental.pallas import tpu as pltpu
from jax.sharding import PartitionSpec as P

CYCLE = 3
RING = 4
MESH = pl.DeviceIdType.MESH
NT = (((1,), (1,)), ((), ()))
X, Y, Z = 0, 1, 2


def kernel(
    blocks,
    scale,
    x_ref,
    occ_ref,
    vir_ref,
    acc,
    vv_ref,
    held,
    raw,
    relay,
    back,
    own_t,
    vv,
    amp,
    amp_b,
    tilde,
    vir_col,
    halves,
    half_in,
    first_in,
    second,
    second_in,
    third,
    third_in,
    local_sem,
    send_sem,
    recv_sem,
    raw_sem,
    relay_sem,
    back_send,
    back_recv,
    vv_send,
    vv_recv,
):
    piece = x_ref.shape[1]
    b, q = lax.axis_index("blk"), lax.axis_index("quarter")
    col, h, l, k = b // 2, lax.rem(b, 2), q // 2, lax.rem(q, 2)
    cx, cz = col // RING, lax.rem(col, RING)
    near = [q, 2 * l + 1 - k, 2 * (1 - l) + k, 2 * (1 - l) + 1 - k]
    ahead, behind = lax.rem(b + 2, blocks), lax.rem(b + blocks - 2, blocks)
    across = 2 * col + 1 - h

    def along_z(step):
        return 2 * (cx * RING + lax.rem(cz + step, RING)) + h

    def along_x(step):
        return 2 * (lax.rem(cx + step, RING) * RING + cz) + h

    barrier = pltpu.get_barrier_semaphore()
    peers = [(b, near[d]) for d in (1, 2, 3)] + [(across, near[d]) for d in range(4)] + [(ahead, q), (behind, q)]
    peers += [(along_z(s), q) for s in (1, 2, 3)] + [(along_x(s), q) for s in (1, 2, 3)]
    for peer in peers:
        pl.semaphore_signal(barrier, inc=1, device_id=peer, device_id_type=MESH)

    def slot(which, j, p):
        return held.at[which * 2 + j, pl.ds(pl.multiple_of(p * piece, piece), piece), :]

    sends = {0: 0, 1: 0}

    def send(side, src, dst, sem, device):
        n = sends[side]
        copy = pltpu.make_async_remote_copy(
            src_ref=src, dst_ref=dst, send_sem=send_sem.at[n], recv_sem=sem, device_id=device, device_id_type=MESH
        )
        copy.start()
        sends[side] = n + 1

    def to_slot(side, src, which, j, p, device):
        send(side, src, slot(which, j, p), recv_sem.at[which, j, p], device)

    def arrived(dst, sem):
        pltpu.make_async_remote_copy(
            src_ref=dst, dst_ref=dst, send_sem=send_sem.at[0], recv_sem=sem, device_id=(b, near[1]), device_id_type=MESH
        ).wait_recv()

    def slot_arrived(which, j, p):
        arrived(slot(which, j, p), recv_sem.at[which, j, p])

    def mine(r, j):
        return x_ref.at[2 * r + j]

    own_copies = [pltpu.make_async_copy(mine(q, j), slot(X, j, q), local_sem.at[j]) for j in range(2)]
    for copy in own_copies:
        copy.start()
    pl.semaphore_wait(barrier, len(peers))

    odd = lax.rem(cz, 2)
    halfway = jnp.where(odd == 1, along_z(2), along_z(3))

    def send_back(side, src, n):
        send(side, src, back.at[odd, n], back_recv.at[odd, n], (halfway, q))

    @pl.when(h == 0)
    def _():
        for d in (1, 2, 3):
            to_slot(0, mine(near[d], 0), X, 0, q, (b, near[d]))
        to_slot(0, mine(near[1], 1), X, 1, q, (b, near[1]))
        to_slot(0, mine(q, 0), Y, 0, q, (ahead, q))
        send_back(0, mine(q, 1), 0)
        for d in (2, 3):
            to_slot(0, mine(near[d], 0), Y, 0, q, (across, near[d]))
        for d in (2, 3):
            to_slot(0, mine(near[d], 1), X, 1, q, (b, near[d]))
        for d in (2, 3):
            to_slot(0, mine(near[d], 1), Y, 1, q, (across, near[d]))
        for j in range(2):
            for d in (0, 1):
                to_slot(0, mine(near[d], j), Y, j, q, (across, near[d]))

    @pl.when(h == 1)
    def _():
        for d in (2, 3):
            send(1, mine(near[d], 1), relay.at[d - 2], relay_sem.at[d - 2], (across, near[d]))
        for d in (1, 2, 3):
            to_slot(1, mine(near[d], 0), X, 0, q, (b, near[d]))
        to_slot(1, mine(near[1], 1), X, 1, q, (b, near[1]))
        to_slot(1, mine(q, 0), Z, 0, q, (ahead, q))
        send_back(1, mine(near[1], 0), 0)
        for d in (2, 3):
            send(1, mine(near[d], 0), raw.at[0, d - 1], raw_sem.at[0, d - 1], (ahead, q))
        to_slot(1, mine(q, 1), Z, 1, q, (ahead, q))
        send_back(1, mine(near[1], 1), 1)

    acc[...] = jnp.zeros_like(acc)
    vv[...] = jnp.zeros_like(vv)
    vir_col[...] = jnp.transpose(jnp.broadcast_to(vir_ref[...], (128, vir_ref.shape[1])))

    def own_piece(j, d):
        slot_arrived(X, j, near[d])

        @pl.when(h == 0)
        def _():
            if (j, d) == (1, 1):
                send_back(0, slot(X, j, near[d]), 1)
            else:
                to_slot(0, slot(X, j, near[d]), Y, j, near[d], (ahead, q))

        if d > 1:

            @pl.when(h == 1)
            def _():
                to_slot(1, slot(X, j, near[d]), Z, j, near[d], (ahead, q))

    def passed_on(j, d):
        @pl.when(h == 1)
        def _():
            if d == 0:
                slot_arrived(Z, j, q)
                to_slot(1, slot(Z, j, q), Z, j, q, (across, q))
                if j == 0:
                    for own in (2, 3):
                        to_slot(1, mine(near[own], 1), X, 1, q, (b, near[own]))
                return
            src = raw.at[j, d - 1]
            arrived(src, raw_sem.at[j, d - 1])
            to_slot(1, src, Z, j, q, (across, near[d]))
            if d == 1:
                to_slot(1, src, Z, j, q, (b, near[d]))

    def relayed():
        @pl.when(h == 0)
        def _():
            for d in (2, 3):
                arrived(relay.at[d - 2], relay_sem.at[d - 2])
                to_slot(0, relay.at[d - 2], Z, 1, near[d], (ahead, q))

    def handed_back(n, act):
        for e in (0, 1):
            source = cx * RING + lax.rem(cz + 1 + e, RING)
            device = (lax.rem(2 * source + 2 + h, blocks), q)
            copy = functools.partial(
                pltpu.make_async_remote_copy,
                src_ref=back.at[e, n], send_sem=back_send.at[e, n], device_id=device, device_id_type=MESH,
            )
            to_raw = copy(dst_ref=raw.at[n, 0], recv_sem=raw_sem.at[n, 0])
            if act == "wait":

                @pl.when(odd == 1)
                def _():
                    to_raw.wait_send()

                continue

            @pl.when(odd == 1)
            def _():
                arrived(back.at[e, n], back_recv.at[e, n])

            @pl.when(jnp.logical_and(odd == 1, h == 1))
            def _():
                to_raw.start()

            p = near[n]

            @pl.when(jnp.logical_and(odd == 1, h == 0))
            def _():
                copy(dst_ref=slot(Y, 1, p), recv_sem=recv_sem.at[Y, 1, p]).start()

    def last_piece(j):
        @pl.when(h == 0)
        def _():
            slot_arrived(Z, j, q)

        for d in (1, 2, 3):
            slot_arrived(Z, j, near[d])

    def turned(i):
        for n in range(held.shape[1] // 256):
            rows = pl.ds(n * 256, 256)
            own_t[i, :, rows] = jnp.transpose(held[2 * X + i, rows, :])

    def before(t):
        @pl.when(t == 1)
        def _():
            passed_on(0, 3)
            handed_back(0, "start")
            own_piece(1, 2)
            passed_on(1, 0)
            handed_back(1, "start")
            own_piece(1, 3)
            relayed()
            turned(1)

        @pl.when(t == 3)
        def _():
            passed_on(0, 1)

        @pl.when(t == 4)
        def _():
            for p in range(4):
                slot_arrived(Y, 0, p)

        @pl.when(t == 5)
        def _():
            passed_on(1, 1)

        @pl.when(t == 6)
        def _():
            last_piece(0)

        @pl.when(t == 8)
        def _():
            for p in range(4):
                slot_arrived(Y, 1, p)

        @pl.when(t == 10)
        def _():
            last_piece(1)

    for copy in own_copies:
        copy.wait()
    own_piece(0, 1)
    own_piece(1, 1)
    own_piece(0, 2)
    passed_on(0, 0)
    own_piece(0, 3)
    passed_on(0, 2)
    turned(0)

    size = vir_ref.shape[1]

    pairs, late = 4 * CYCLE, tilde.shape[0]

    def place(t):
        turn = t // 2
        which = jnp.where(turn < 2, X, Y + lax.rem(turn, 2))
        j = jnp.where(turn < 2, turn, (turn - 2) // 2)
        return lax.rem(t, 2), which, j

    def to_gamma(t):
        i, which, j = place(t)
        other = held.at[which * 2 + j]
        for n in range(held.shape[1] // 256):
            rows = pl.ds(n * 256, 256)
            acc[i, :, rows] += lax.dot_general(tilde[lax.rem(t, late)], other[rows, :], NT, preferred_element_type=jnp.float32)

    def pair(t, carry):
        before(t)
        i, which, j = place(t)
        behind_by = jnp.where(which == X, 0, jnp.where(which == Y, 2 - h, 1 + h))
        partner = lax.rem(b - behind_by + blocks, blocks)
        e_i = occ_ref[(b * 4 + q) * 2 + i]
        e_j = occ_ref[(partner * 4 + q) * 2 + j]
        other = held.at[which * 2 + j]
        for n in range(size // 256):
            cols = pl.ds(n * 256, 256)
            pairint = jnp.dot(own_t[i], other[:, cols], preferred_element_type=jnp.float32)
            for m in range(2):
                lanes = pl.ds(n * 256 + m * 128, 128)
                denom = vir_col[...] + vir_ref[:, lanes] - e_i - e_j
                ratio = pairint[:, m * 128 : (m + 1) * 128] / denom
                amp[:, lanes] = ratio
                amp_b[:, lanes] = ratio.astype(jnp.bfloat16)
        for n in range(size // 128):
            rows = pl.ds(n * 128, 128)
            tilde[lax.rem(t, late), rows, :] = (2.0 * amp[rows, :] - jnp.transpose(amp[:, rows])).astype(jnp.bfloat16)
        vv[...] += lax.dot_general(amp_b[...], tilde[lax.rem(t, late)], NT, preferred_element_type=jnp.float32)

        @pl.when(t < pairs - late)
        def _():
            to_gamma(t)

        return carry

    lax.fori_loop(0, pairs, pair, 0)

    low = lax.broadcasted_iota(jnp.int32, (8, 256), 0) < 4
    square = RING * RING
    for chip in range(size // 8):
        spot = (chip % RING) * square + ((chip // RING) % RING) * RING + chip // square
        rows = pl.ds(chip * 8, 8)
        left, right = vv[rows, 0:256], vv[rows, 256:512]
        for core, block in enumerate((jnp.where(low, left, pltpu.roll(right, 4, 0)), jnp.where(low, pltpu.roll(left, 4, 0), right))):
            halves[core, 0, spot] = block[:, 0:128]
            halves[core, 1, chip] = block[:, 128:256]

    swap = pltpu.make_async_remote_copy(
        src_ref=halves.at[1 - k], dst_ref=half_in, send_sem=vv_send.at[0], recv_sem=vv_recv.at[0],
        device_id=(b, near[1]), device_id_type=MESH,
    )
    swap.start()
    to_gamma(pairs - 4)
    to_gamma(pairs - 3)
    swap.wait()
    half_in[...] += halves[k]

    here = 2 * h + l
    column = []
    for s in (1, 2, 3):
        there = lax.rem(here + s, RING)
        column.append((2 * col + there // 2, 2 * lax.rem(there, 2) + k))
    rings = {
        "y": (here, column),
        "z": (cz, [(along_z(s), q) for s in (1, 2, 3)]),
        "x": (cx, [(along_x(s), q) for s in (1, 2, 3)]),
    }

    def stage(src, landing, first, axis):
        me, devices = rings[axis]
        copies = [
            pltpu.make_async_remote_copy(
                src_ref=src.at[lax.rem(me + s, RING)], dst_ref=landing.at[s - 1],
                send_sem=vv_send.at[first + s - 1], recv_sem=vv_recv.at[first + s - 1],
                device_id=devices[s - 1], device_id_type=MESH,
            )
            for s in (1, 2, 3)
        ]
        for copy in copies:
            copy.start()

        def total():
            for copy in copies:
                copy.wait()
            return src[me] + landing[0] + landing[1] + landing[2]

        return total

    orders = ("yzx", "xzy")
    waits = [stage(half_in.at[n].reshape(RING, square, 8, 128), first_in.at[n], 1 + 3 * n, orders[n][0]) for n in range(2)]
    to_gamma(pairs - 2)
    to_gamma(pairs - 1)
    for n in range(2):
        second[n] = waits[n]()
        waits[n] = stage(second.at[n].reshape(RING, RING, 8, 128), second_in.at[n], 7 + 3 * n, orders[n][1])
    for n in range(2):
        third[n] = waits[n]()
        waits[n] = stage(third.at[n], third_in.at[n], 13 + 3 * n, orders[n][2])
    for n in range(2):
        total = waits[n]() * scale
        lanes = pl.ds(n * 128, 128)
        vv_ref[:, lanes] = total[0:4]
        vv_ref[:, pl.ds(256 + n * 128, 128)] = total[4:8]

    for n in range(2):
        handed_back(n, "wait")
    for side in (0, 1):

        @pl.when(h == side)
        def _():
            for n in range(sends[side]):
                pltpu.make_async_remote_copy(
                    src_ref=x_ref.at[0], dst_ref=raw.at[0, 0], send_sem=send_sem.at[n], recv_sem=recv_sem.at[0, 0, 0],
                    device_id=(b, near[1]), device_id_type=MESH,
                ).wait_send()


def per_device(blocks, quarters, bints, occ_energy, vir_energy):
    rows, size, piece = bints.shape
    naux = piece * quarters
    pair_rows = rows // quarters
    f32, bf16 = jnp.float32, jnp.bfloat16
    scale = 1.0 / float(pair_rows * blocks * quarters * CYCLE * pair_rows)
    dma = pltpu.SemaphoreType.DMA
    chips = size // 8
    return pl.pallas_call(
        functools.partial(kernel, blocks, scale),
        out_shape=(
            jax.ShapeDtypeStruct((pair_rows, size, naux), f32),
            jax.ShapeDtypeStruct((size // (blocks * quarters), size), f32),
        ),
        in_specs=[
            pl.BlockSpec(memory_space=pltpu.HBM),
            pl.BlockSpec(memory_space=pltpu.SMEM),
            pl.BlockSpec(memory_space=pltpu.VMEM),
        ],
        out_specs=(pl.BlockSpec(memory_space=pltpu.VMEM), pl.BlockSpec(memory_space=pltpu.VMEM)),
        scratch_shapes=[
            pltpu.VMEM((3 * pair_rows, naux, size), bf16),
            pltpu.VMEM((pair_rows, 3, piece, size), bf16),
            pltpu.VMEM((2, piece, size), bf16),
            pltpu.VMEM((2, 2, piece, size), bf16),
            pltpu.VMEM((pair_rows, size, naux), bf16),
            pltpu.VMEM((size, size), f32),
            pltpu.VMEM((size, size), f32),
            pltpu.VMEM((size, size), bf16),
            pltpu.VMEM((4, size, size), bf16),
            pltpu.VMEM((size, 128), f32),
            pltpu.VMEM((2, 2, chips, 8, 128), f32),
            pltpu.VMEM((2, chips, 8, 128), f32),
            pltpu.VMEM((2, 3, 16, 8, 128), f32),
            pltpu.VMEM((2, 16, 8, 128), f32),
            pltpu.VMEM((2, 3, 4, 8, 128), f32),
            pltpu.VMEM((2, 4, 8, 128), f32),
            pltpu.VMEM((2, 3, 8, 128), f32),
            dma((2,)),
            dma((40,)),
            dma((3, 2, 4)),
            dma((2, 3)),
            dma((2,)),
            dma((2, 2)),
            dma((2, 2)),
            dma((19,)),
            dma((19,)),
        ],
        compiler_params=pltpu.CompilerParams(
            collective_id=0, has_side_effects=True, vmem_limit_bytes=40 * 2**20
        ),
        name="pair_densities",
    )(pltpu.with_memory_space_constraint(jnp.swapaxes(bints, 1, 2), pltpu.HBM), pltpu.with_memory_space_constraint(occ_energy, pltpu.HBM), pltpu.with_memory_space_constraint(vir_energy.reshape(1, size), pltpu.HBM))


def solution(mesh):
    return jax.shard_map(
        functools.partial(per_device, mesh.shape["blk"], mesh.shape["quarter"]),
        mesh=mesh,
        in_specs=(P("blk", None, "quarter"), P(), P()),
        out_specs=(P(("blk", "quarter"), None, None), P(("blk", "quarter"), None)),
        check_vma=False,
    )
```

```python
import functools

import jax
import jax.numpy as jnp
from jax import lax
from jax.experimental import pallas as pl
from jax.experimental.pallas import tpu as pltpu
from jax.sharding import PartitionSpec as P

CYCLE = 3
RING = 4
MESH = pl.DeviceIdType.MESH
NT = (((1,), (1,)), ((), ()))
X, Y, Z = 0, 1, 2


def kernel(
    blocks,
    scale,
    x_ref,
    occ_ref,
    vir_ref,
    acc,
    vv_ref,
    held,
    raw,
    relay,
    back,
    own_t,
    vv,
    amp,
    amp_b,
    tilde,
    vir_col,
    halves,
    half_in,
    parts,
    local_sem,
    send_sem,
    recv_sem,
    raw_sem,
    relay_sem,
    back_send,
    back_recv,
    vv_send,
    vv_recv,
    known,
):
    piece = x_ref.shape[1]
    b, q = lax.axis_index("blk"), lax.axis_index("quarter")
    col, h, l, k = b // 2, lax.rem(b, 2), q // 2, lax.rem(q, 2)
    cx, cz = col // RING, lax.rem(col, RING)
    near = [q, 2 * l + 1 - k, 2 * (1 - l) + k, 2 * (1 - l) + 1 - k]
    ahead, behind = lax.rem(b + 2, blocks), lax.rem(b + blocks - 2, blocks)
    across = 2 * col + 1 - h

    def along_z(step):
        return 2 * (cx * RING + lax.rem(cz + step, RING)) + h

    def along_x(step):
        return 2 * (lax.rem(cx + step, RING) * RING + cz) + h

    barrier = pltpu.get_barrier_semaphore()
    peers = [(b, near[d]) for d in (1, 2, 3)] + [(across, near[d]) for d in range(4)] + [(ahead, q), (behind, q)]
    peers += [(along_z(s), q) for s in (1, 2, 3)] + [(along_x(s), q) for s in (1, 2, 3)]
    for peer in peers:
        pl.semaphore_signal(barrier, inc=1, device_id=peer, device_id_type=MESH)

    def slot(which, j, p):
        return held.at[which * 2 + j, pl.ds(pl.multiple_of(p * piece, piece), piece), :]

    sends = {0: 0, 1: 0}

    def send(side, src, dst, sem, device):
        n = sends[side]
        copy = pltpu.make_async_remote_copy(
            src_ref=src, dst_ref=dst, send_sem=send_sem.at[n], recv_sem=sem, device_id=device, device_id_type=MESH
        )
        copy.start()
        sends[side] = n + 1

    def to_slot(side, src, which, j, p, device):
        send(side, src, slot(which, j, p), recv_sem.at[which, j, p], device)

    def arrived(dst, sem):
        pltpu.make_async_remote_copy(
            src_ref=dst, dst_ref=dst, send_sem=send_sem.at[0], recv_sem=sem, device_id=(b, near[1]), device_id_type=MESH
        ).wait_recv()

    def slot_arrived(which, j, p):
        arrived(slot(which, j, p), recv_sem.at[which, j, p])

    def mine(r, j):
        return x_ref.at[2 * r + j]

    own_copies = [pltpu.make_async_copy(mine(q, j), slot(X, j, q), local_sem.at[j]) for j in range(2)]
    for copy in own_copies:
        copy.start()
    pl.semaphore_wait(barrier, len(peers))

    odd = lax.rem(cz, 2)
    halfway = jnp.where(odd == 1, along_z(2), along_z(3))

    def send_back(side, src, n):
        send(side, src, back.at[odd, n], back_recv.at[odd, n], (halfway, q))

    @pl.when(h == 0)
    def _():
        for d in (1, 2, 3):
            to_slot(0, mine(near[d], 0), X, 0, q, (b, near[d]))
        to_slot(0, mine(near[1], 1), X, 1, q, (b, near[1]))
        to_slot(0, mine(q, 0), Y, 0, q, (ahead, q))
        send_back(0, mine(q, 1), 0)
        for d in (2, 3):
            to_slot(0, mine(near[d], 0), Y, 0, q, (across, near[d]))
        for d in (2, 3):
            to_slot(0, mine(near[d], 1), X, 1, q, (b, near[d]))
        for d in (2, 3):
            to_slot(0, mine(near[d], 1), Y, 1, q, (across, near[d]))
        for j in range(2):
            for d in (0, 1):
                to_slot(0, mine(near[d], j), Y, j, q, (across, near[d]))

    @pl.when(h == 1)
    def _():
        for d in (2, 3):
            send(1, mine(near[d], 1), relay.at[d - 2], relay_sem.at[d - 2], (across, near[d]))
        for d in (1, 2, 3):
            to_slot(1, mine(near[d], 0), X, 0, q, (b, near[d]))
        to_slot(1, mine(near[1], 1), X, 1, q, (b, near[1]))
        to_slot(1, mine(q, 0), Z, 0, q, (ahead, q))
        send_back(1, mine(near[1], 0), 0)
        for d in (2, 3):
            send(1, mine(near[d], 0), raw.at[0, d - 1], raw_sem.at[0, d - 1], (ahead, q))
        to_slot(1, mine(q, 1), Z, 1, q, (ahead, q))
        send_back(1, mine(near[1], 1), 1)

    for s in (1, 2, 3):
        pl.semaphore_signal(known.at[0], inc=1, device_id=(along_z(s), q), device_id_type=MESH)
    acc[...] = jnp.zeros_like(acc)
    vv[...] = jnp.zeros_like(vv)
    vir_col[...] = jnp.transpose(jnp.broadcast_to(vir_ref[...], (128, vir_ref.shape[1])))

    def own_piece(j, d):
        slot_arrived(X, j, near[d])

        @pl.when(h == 0)
        def _():
            if (j, d) == (1, 1):
                send_back(0, slot(X, j, near[d]), 1)
            else:
                to_slot(0, slot(X, j, near[d]), Y, j, near[d], (ahead, q))

        if d > 1:

            @pl.when(h == 1)
            def _():
                to_slot(1, slot(X, j, near[d]), Z, j, near[d], (ahead, q))

    def passed_on(j, d):
        @pl.when(h == 1)
        def _():
            if d == 0:
                slot_arrived(Z, j, q)
                to_slot(1, slot(Z, j, q), Z, j, q, (across, q))
                if j == 0:
                    for own in (2, 3):
                        to_slot(1, mine(near[own], 1), X, 1, q, (b, near[own]))
                return
            src = raw.at[j, d - 1]
            arrived(src, raw_sem.at[j, d - 1])
            to_slot(1, src, Z, j, q, (across, near[d]))
            if d == 1:
                to_slot(1, src, Z, j, q, (b, near[d]))

    def relayed():
        @pl.when(h == 0)
        def _():
            for d in (2, 3):
                arrived(relay.at[d - 2], relay_sem.at[d - 2])
                to_slot(0, relay.at[d - 2], Z, 1, near[d], (ahead, q))

    def handed_back(n, act):
        for e in (0, 1):
            source = cx * RING + lax.rem(cz + 1 + e, RING)
            device = (lax.rem(2 * source + 2 + h, blocks), q)
            copy = functools.partial(
                pltpu.make_async_remote_copy,
                src_ref=back.at[e, n], send_sem=back_send.at[e, n], device_id=device, device_id_type=MESH,
            )
            to_raw = copy(dst_ref=raw.at[n, 0], recv_sem=raw_sem.at[n, 0])
            if act == "wait":

                @pl.when(odd == 1)
                def _():
                    to_raw.wait_send()

                continue

            @pl.when(odd == 1)
            def _():
                arrived(back.at[e, n], back_recv.at[e, n])

            @pl.when(jnp.logical_and(odd == 1, h == 1))
            def _():
                to_raw.start()

            p = near[n]

            @pl.when(jnp.logical_and(odd == 1, h == 0))
            def _():
                copy(dst_ref=slot(Y, 1, p), recv_sem=recv_sem.at[Y, 1, p]).start()

    def last_piece(j):
        @pl.when(h == 0)
        def _():
            slot_arrived(Z, j, q)

        for d in (1, 2, 3):
            slot_arrived(Z, j, near[d])

    def turned(i):
        for n in range(held.shape[1] // 256):
            rows = pl.ds(n * 256, 256)
            own_t[i, :, rows] = jnp.transpose(held[2 * X + i, rows, :])

    def before(t):
        @pl.when(t == 1)
        def _():
            passed_on(0, 3)
            handed_back(0, "start")
            own_piece(1, 2)
            passed_on(1, 0)
            handed_back(1, "start")
            own_piece(1, 3)
            relayed()
            turned(1)

        @pl.when(t == 3)
        def _():
            passed_on(0, 1)

        @pl.when(t == 4)
        def _():
            for p in range(4):
                slot_arrived(Y, 0, p)

        @pl.when(t == 5)
        def _():
            passed_on(1, 1)

        @pl.when(t == 6)
        def _():
            last_piece(0)

        @pl.when(t == 8)
        def _():
            for p in range(4):
                slot_arrived(Y, 1, p)

        @pl.when(t == 10)
        def _():
            last_piece(1)

    for copy in own_copies:
        copy.wait()
    own_piece(0, 1)
    own_piece(1, 1)
    own_piece(0, 2)
    passed_on(0, 0)
    own_piece(0, 3)
    passed_on(0, 2)
    pl.semaphore_wait(known.at[0], 3)
    for s in (1, 2, 3):
        pl.semaphore_signal(known.at[1], inc=1, device_id=(along_x(s), q), device_id_type=MESH)
    turned(0)

    size = vir_ref.shape[1]

    pairs, late = 4 * CYCLE, tilde.shape[0]

    def place(t):
        turn = t // 2
        which = jnp.where(turn < 2, X, Y + lax.rem(turn, 2))
        j = jnp.where(turn < 2, turn, (turn - 2) // 2)
        return lax.rem(t, 2), which, j

    def to_gamma(t):
        i, which, j = place(t)
        other = held.at[which * 2 + j]
        for n in range(held.shape[1] // 256):
            rows = pl.ds(n * 256, 256)
            acc[i, :, rows] += lax.dot_general(tilde[lax.rem(t, late)], other[rows, :], NT, preferred_element_type=jnp.float32)

    def pair(t, carry):
        before(t)
        i, which, j = place(t)
        behind_by = jnp.where(which == X, 0, jnp.where(which == Y, 2 - h, 1 + h))
        partner = lax.rem(b - behind_by + blocks, blocks)
        e_i = occ_ref[(b * 4 + q) * 2 + i]
        e_j = occ_ref[(partner * 4 + q) * 2 + j]
        other = held.at[which * 2 + j]
        for n in range(size // 256):
            cols = pl.ds(n * 256, 256)
            pairint = jnp.dot(own_t[i], other[:, cols], preferred_element_type=jnp.float32)
            for m in range(2):
                lanes = pl.ds(n * 256 + m * 128, 128)
                denom = vir_col[...] + vir_ref[:, lanes] - e_i - e_j
                ratio = pairint[:, m * 128 : (m + 1) * 128] / denom
                amp[:, lanes] = ratio
                amp_b[:, lanes] = ratio.astype(jnp.bfloat16)
        for n in range(size // 128):
            rows = pl.ds(n * 128, 128)
            tilde[lax.rem(t, late), rows, :] = (2.0 * amp[rows, :] - jnp.transpose(amp[:, rows])).astype(jnp.bfloat16)
        vv[...] += lax.dot_general(amp_b[...], tilde[lax.rem(t, late)], NT, preferred_element_type=jnp.float32)

        @pl.when(t < pairs - late)
        def _():
            to_gamma(t)

        return carry

    lax.fori_loop(0, pairs, pair, 0)

    low = lax.broadcasted_iota(jnp.int32, (8, 256), 0) < 4
    for chip in range(size // 8):
        rows = pl.ds(chip * 8, 8)
        left, right = vv[rows, 0:256], vv[rows, 256:512]
        halves[0, chip] = jnp.where(low, left, pltpu.roll(right, 4, 0))
        halves[1, chip] = jnp.where(low, pltpu.roll(left, 4, 0), right)

    swap = pltpu.make_async_remote_copy(
        src_ref=halves.at[1 - k], dst_ref=half_in, send_sem=vv_send.at[0], recv_sem=vv_recv.at[0],
        device_id=(b, near[1]), device_id_type=MESH,
    )
    swap.start()
    to_gamma(pairs - 6)
    to_gamma(pairs - 5)
    pl.semaphore_wait(known.at[1], 3)
    swap.wait()
    half_in[...] += halves[k]

    here = 2 * h + l
    offsets = [(dx, dz, dy) for dx in range(RING) for dz in range(RING) for dy in range(RING) if dx or dz or dy]
    offsets.sort(key=lambda o: -sum(min(d, RING - d) for d in o))
    turns = {d: (lax.rem(cx + d, RING), lax.rem(cz + d, RING), lax.rem(here + d, RING)) for d in range(RING)}
    for n, (dx, dz, dy) in enumerate(offsets):
        tx, tz, ty = turns[dx][0], turns[dz][1], turns[dy][2]
        column = tx * RING + tz
        pltpu.make_async_remote_copy(
            src_ref=half_in.at[column * RING + ty], dst_ref=parts.at[n], send_sem=vv_send.at[1], recv_sem=vv_recv.at[1],
            device_id=(2 * column + ty // 2, 2 * lax.rem(ty, 2) + k), device_id_type=MESH,
        ).start()
    for n in (4, 3, 2, 1):
        to_gamma(pairs - n)
    everything = pltpu.make_async_remote_copy(
        src_ref=parts, dst_ref=parts, send_sem=vv_send.at[1], recv_sem=vv_recv.at[1],
        device_id=(b, near[1]), device_id_type=MESH,
    )
    everything.wait_recv()
    total = (half_in[(cx * RING + cz) * RING + here] + jnp.sum(parts[...], axis=0)) * scale
    vv_ref[:, 0:256] = total[0:4]
    vv_ref[:, 256:512] = total[4:8]
    everything.wait_send()

    for n in range(2):
        handed_back(n, "wait")
    for side in (0, 1):

        @pl.when(h == side)
        def _():
            for n in range(sends[side]):
                pltpu.make_async_remote_copy(
                    src_ref=x_ref.at[0], dst_ref=raw.at[0, 0], send_sem=send_sem.at[n], recv_sem=recv_sem.at[0, 0, 0],
                    device_id=(b, near[1]), device_id_type=MESH,
                ).wait_send()


def per_device(blocks, quarters, bints, occ_energy, vir_energy):
    rows, size, piece = bints.shape
    naux = piece * quarters
    pair_rows = rows // quarters
    f32, bf16 = jnp.float32, jnp.bfloat16
    scale = 1.0 / float(pair_rows * blocks * quarters * CYCLE * pair_rows)
    dma = pltpu.SemaphoreType.DMA
    chips = size // 8
    return pl.pallas_call(
        functools.partial(kernel, blocks, scale),
        out_shape=(
            jax.ShapeDtypeStruct((pair_rows, size, naux), f32),
            jax.ShapeDtypeStruct((size // (blocks * quarters), size), f32),
        ),
        in_specs=[
            pl.BlockSpec(memory_space=pltpu.HBM),
            pl.BlockSpec(memory_space=pltpu.SMEM),
            pl.BlockSpec(memory_space=pltpu.VMEM),
        ],
        out_specs=(pl.BlockSpec(memory_space=pltpu.VMEM), pl.BlockSpec(memory_space=pltpu.VMEM)),
        scratch_shapes=[
            pltpu.VMEM((3 * pair_rows, naux, size), bf16),
            pltpu.VMEM((pair_rows, 3, piece, size), bf16),
            pltpu.VMEM((2, piece, size), bf16),
            pltpu.VMEM((2, 2, piece, size), bf16),
            pltpu.VMEM((pair_rows, size, naux), bf16),
            pltpu.VMEM((size, size), f32),
            pltpu.VMEM((size, size), f32),
            pltpu.VMEM((size, size), bf16),
            pltpu.VMEM((6, size, size), bf16),
            pltpu.VMEM((size, 128), f32),
            pltpu.VMEM((2, chips, 8, 256), f32),
            pltpu.VMEM((chips, 8, 256), f32),
            pltpu.VMEM((chips - 1, 8, 256), f32),
            dma((2,)),
            dma((40,)),
            dma((3, 2, 4)),
            dma((2, 3)),
            dma((2,)),
            dma((2, 2)),
            dma((2, 2)),
            dma((2,)),
            dma((2,)),
            pltpu.SemaphoreType.REGULAR((2,)),
        ],
        compiler_params=pltpu.CompilerParams(
            collective_id=0, has_side_effects=True, vmem_limit_bytes=40 * 2**20
        ),
        name="pair_densities",
    )(pltpu.with_memory_space_constraint(jnp.swapaxes(bints, 1, 2), pltpu.HBM), pltpu.with_memory_space_constraint(occ_energy, pltpu.HBM), pltpu.with_memory_space_constraint(vir_energy.reshape(1, size), pltpu.HBM))


def solution(mesh):
    return jax.shard_map(
        functools.partial(per_device, mesh.shape["blk"], mesh.shape["quarter"]),
        mesh=mesh,
        in_specs=(P("blk", None, "quarter"), P(), P()),
        out_specs=(P(("blk", "quarter"), None, None), P(("blk", "quarter"), None)),
        check_vma=False,
    )
```

```python
import functools

import jax
import jax.numpy as jnp
from jax import lax
from jax.experimental import pallas as pl
from jax.experimental.pallas import tpu as pltpu
from jax.sharding import PartitionSpec as P

CYCLE = 3
RING = 4
MESH = pl.DeviceIdType.MESH
NT = (((1,), (1,)), ((), ()))
X, Y, Z = 0, 1, 2


def kernel(
    blocks,
    scale,
    x_ref,
    occ_ref,
    vir_ref,
    acc,
    vv_ref,
    held,
    raw,
    relay,
    back,
    own_t,
    vv,
    amp,
    amp_b,
    tilde,
    vir_col,
    halves,
    half_in,
    parts,
    local_sem,
    send_sem,
    recv_sem,
    raw_sem,
    relay_sem,
    back_send,
    back_recv,
    vv_send,
    vv_recv,
    known,
):
    piece = x_ref.shape[1]
    b, q = lax.axis_index("blk"), lax.axis_index("quarter")
    col, h, l, k = b // 2, lax.rem(b, 2), q // 2, lax.rem(q, 2)
    cx, cz = col // RING, lax.rem(col, RING)
    near = [q, 2 * l + 1 - k, 2 * (1 - l) + k, 2 * (1 - l) + 1 - k]
    ahead, behind = lax.rem(b + 2, blocks), lax.rem(b + blocks - 2, blocks)
    across = 2 * col + 1 - h

    def along_z(step):
        return 2 * (cx * RING + lax.rem(cz + step, RING)) + h

    def along_x(step):
        return 2 * (lax.rem(cx + step, RING) * RING + cz) + h

    barrier = pltpu.get_barrier_semaphore()
    peers = [(b, near[d]) for d in (1, 2, 3)] + [(across, near[d]) for d in range(4)] + [(ahead, q), (behind, q)]
    peers += [(along_z(s), q) for s in (1, 2, 3)] + [(along_x(s), q) for s in (1, 2, 3)]
    for peer in peers:
        pl.semaphore_signal(barrier, inc=1, device_id=peer, device_id_type=MESH)

    def slot(which, j, p):
        return held.at[which * 2 + j, pl.ds(pl.multiple_of(p * piece, piece), piece), :]

    sends = {0: 0, 1: 0}

    def send(side, src, dst, sem, device):
        n = sends[side]
        copy = pltpu.make_async_remote_copy(
            src_ref=src, dst_ref=dst, send_sem=send_sem.at[n], recv_sem=sem, device_id=device, device_id_type=MESH
        )
        copy.start()
        sends[side] = n + 1

    def to_slot(side, src, which, j, p, device):
        send(side, src, slot(which, j, p), recv_sem.at[which, j, p], device)

    def arrived(dst, sem):
        pltpu.make_async_remote_copy(
            src_ref=dst, dst_ref=dst, send_sem=send_sem.at[0], recv_sem=sem, device_id=(b, near[1]), device_id_type=MESH
        ).wait_recv()

    def slot_arrived(which, j, p):
        arrived(slot(which, j, p), recv_sem.at[which, j, p])

    def mine(r, j):
        return x_ref.at[2 * r + j]

    own_copies = [pltpu.make_async_copy(mine(q, j), slot(X, j, q), local_sem.at[j]) for j in range(2)]
    for copy in own_copies:
        copy.start()
    pl.semaphore_wait(barrier, len(peers))

    odd = lax.rem(cz, 2)
    halfway = jnp.where(odd == 1, along_z(2), along_z(3))

    def send_back(side, src, n):
        send(side, src, back.at[odd, n], back_recv.at[odd, n], (halfway, q))

    @pl.when(h == 0)
    def _():
        for d in (1, 2, 3):
            to_slot(0, mine(near[d], 0), X, 0, q, (b, near[d]))
        to_slot(0, mine(near[1], 1), X, 1, q, (b, near[1]))
        to_slot(0, mine(q, 0), Y, 0, q, (ahead, q))
        send_back(0, mine(q, 1), 0)
        for d in (2, 3):
            to_slot(0, mine(near[d], 0), Y, 0, q, (across, near[d]))
        for d in (2, 3):
            to_slot(0, mine(near[d], 1), X, 1, q, (b, near[d]))
        for d in (2, 3):
            to_slot(0, mine(near[d], 1), Y, 1, q, (across, near[d]))
        for j in range(2):
            for d in (0, 1):
                to_slot(0, mine(near[d], j), Y, j, q, (across, near[d]))

    @pl.when(h == 1)
    def _():
        for d in (2, 3):
            send(1, mine(near[d], 1), relay.at[d - 2], relay_sem.at[d - 2], (across, near[d]))
        for d in (1, 2, 3):
            to_slot(1, mine(near[d], 0), X, 0, q, (b, near[d]))
        to_slot(1, mine(near[1], 1), X, 1, q, (b, near[1]))
        to_slot(1, mine(q, 0), Z, 0, q, (ahead, q))
        send_back(1, mine(near[1], 0), 0)
        for d in (2, 3):
            send(1, mine(near[d], 0), raw.at[0, d - 1], raw_sem.at[0, d - 1], (ahead, q))
        to_slot(1, mine(q, 1), Z, 1, q, (ahead, q))
        send_back(1, mine(near[1], 1), 1)

    for s in (1, 2, 3):
        pl.semaphore_signal(known.at[0], inc=1, device_id=(along_z(s), q), device_id_type=MESH)
    acc[...] = jnp.zeros_like(acc)
    vv[...] = jnp.zeros_like(vv)
    vir_col[...] = jnp.transpose(jnp.broadcast_to(vir_ref[...], (128, vir_ref.shape[1])))

    def own_piece(j, d, sides=(0, 1)):
        slot_arrived(X, j, near[d])

        if 0 in sides:

            @pl.when(h == 0)
            def _():
                if (j, d) == (1, 1):
                    send_back(0, slot(X, j, near[d]), 1)
                else:
                    to_slot(0, slot(X, j, near[d]), Y, j, near[d], (ahead, q))

        if d > 1 and 1 in sides:

            @pl.when(h == 1)
            def _():
                to_slot(1, slot(X, j, near[d]), Z, j, near[d], (ahead, q))

    def passed_on(j, d):
        @pl.when(h == 1)
        def _():
            if d == 0:
                slot_arrived(Z, j, q)
                to_slot(1, slot(Z, j, q), Z, j, q, (across, q))
                if j == 0:
                    for own in (2, 3):
                        to_slot(1, mine(near[own], 1), X, 1, q, (b, near[own]))
                return
            src = raw.at[j, d - 1]
            arrived(src, raw_sem.at[j, d - 1])
            to_slot(1, src, Z, j, q, (across, near[d]))
            if d == 1:
                to_slot(1, src, Z, j, q, (b, near[d]))

    def relayed():
        @pl.when(h == 0)
        def _():
            for d in (2, 3):
                arrived(relay.at[d - 2], relay_sem.at[d - 2])
                to_slot(0, relay.at[d - 2], Z, 1, near[d], (ahead, q))

    def handed_back(n, act):
        for e in (0, 1):
            source = cx * RING + lax.rem(cz + 1 + e, RING)
            device = (lax.rem(2 * source + 2 + h, blocks), q)
            copy = functools.partial(
                pltpu.make_async_remote_copy,
                src_ref=back.at[e, n], send_sem=back_send.at[e, n], device_id=device, device_id_type=MESH,
            )
            to_raw = copy(dst_ref=raw.at[n, 0], recv_sem=raw_sem.at[n, 0])
            if act == "wait":

                @pl.when(odd == 1)
                def _():
                    to_raw.wait_send()

                continue

            @pl.when(odd == 1)
            def _():
                arrived(back.at[e, n], back_recv.at[e, n])

            @pl.when(jnp.logical_and(odd == 1, h == 1))
            def _():
                to_raw.start()

            p = near[n]

            @pl.when(jnp.logical_and(odd == 1, h == 0))
            def _():
                copy(dst_ref=slot(Y, 1, p), recv_sem=recv_sem.at[Y, 1, p]).start()

    def last_piece(j):
        @pl.when(h == 0)
        def _():
            slot_arrived(Z, j, q)

        for d in (1, 2, 3):
            slot_arrived(Z, j, near[d])

    def turned(i):
        for n in range(held.shape[1] // 256):
            rows = pl.ds(n * 256, 256)
            own_t[i, :, rows] = jnp.transpose(held[2 * X + i, rows, :])

    def before(turn):
        @pl.when(turn == 1)
        def _():
            passed_on(0, 1)

        @pl.when(turn == 2)
        def _():
            for p in range(4):
                slot_arrived(Y, 0, p)

        @pl.when(turn == 3)
        def _():
            passed_on(1, 1)
            last_piece(0)

        @pl.when(turn == 4)
        def _():
            for p in range(4):
                slot_arrived(Y, 1, p)

        @pl.when(turn == 5)
        def _():
            last_piece(1)

    for copy in own_copies:
        copy.wait()
    own_piece(0, 1)
    own_piece(1, 1)
    own_piece(0, 2)
    passed_on(0, 0)
    own_piece(0, 3)
    passed_on(0, 2)
    pl.semaphore_wait(known.at[0], 3)
    for s in (1, 2, 3):
        pl.semaphore_signal(known.at[1], inc=1, device_id=(along_x(s), q), device_id_type=MESH)
    turned(0)
    passed_on(0, 3)

    @pl.when(h == 0)
    def _():
        own_piece(1, 2, (0,))
        handed_back(0, "start")
        own_piece(1, 3, (0,))

    relayed()

    @pl.when(h == 0)
    def _():
        handed_back(1, "start")

    @pl.when(h == 1)
    def _():
        handed_back(0, "start")
        own_piece(1, 2, (1,))

    passed_on(1, 0)

    @pl.when(h == 1)
    def _():
        handed_back(1, "start")
        own_piece(1, 3, (1,))

    turned(1)

    size = vir_ref.shape[1]

    turns, late = 2 * CYCLE, tilde.shape[0]
    rows_both = 2 * size

    def place(turn):
        which = jnp.where(turn < 2, X, Y + lax.rem(turn, 2))
        return which, jnp.where(turn < 2, turn, (turn - 2) // 2)

    def to_gamma(turn):
        which, j = place(turn)
        other = held.at[which * 2 + j]
        both = tilde[lax.rem(turn, late)].reshape(rows_both, size)
        for n in range(held.shape[1] // 256):
            rows = pl.ds(n * 256, 256)
            terms = lax.dot_general(both, other[rows, :], NT, preferred_element_type=jnp.float32)
            acc[:, :, rows] += terms.reshape(2, size, 256)

    def pairs(turn, carry):
        before(turn)
        which, j = place(turn)
        slot_out = lax.rem(turn, late)
        behind_by = jnp.where(which == X, 0, jnp.where(which == Y, 2 - h, 1 + h))
        partner = lax.rem(b - behind_by + blocks, blocks)
        e_j = occ_ref[(partner * 4 + q) * 2 + j]
        other = held.at[which * 2 + j]
        for n in range(size // 256):
            cols = pl.ds(n * 256, 256)
            pairint = jnp.dot(own_t[...].reshape(rows_both, -1), other[:, cols], preferred_element_type=jnp.float32)
            for i in range(2):
                e_i = occ_ref[(b * 4 + q) * 2 + i]
                for m in range(2):
                    lanes = pl.ds(n * 256 + m * 128, 128)
                    denom = vir_col[...] + vir_ref[:, lanes] - e_i - e_j
                    ratio = pairint[i * size : (i + 1) * size, m * 128 : (m + 1) * 128] / denom
                    amp[i, :, lanes] = ratio
                    amp_b[i, :, lanes] = ratio.astype(jnp.bfloat16)
        for i in range(2):
            for n in range(size // 128):
                rows = pl.ds(n * 128, 128)
                turned_back = jnp.transpose(amp[i, :, rows])
                tilde[slot_out, i, rows, :] = (2.0 * amp[i, rows, :] - turned_back).astype(jnp.bfloat16)
            vv[...] += lax.dot_general(amp_b[i], tilde[slot_out, i], NT, preferred_element_type=jnp.float32)

        @pl.when(turn < turns - late)
        def _():
            to_gamma(turn)

        return carry

    lax.fori_loop(0, turns, pairs, 0)

    low = lax.broadcasted_iota(jnp.int32, (8, 256), 0) < 4
    for chip in range(size // 8):
        rows = pl.ds(chip * 8, 8)
        left, right = vv[rows, 0:256], vv[rows, 256:512]
        halves[0, chip] = jnp.where(low, left, pltpu.roll(right, 4, 0))
        halves[1, chip] = jnp.where(low, pltpu.roll(left, 4, 0), right)

    swap = pltpu.make_async_remote_copy(
        src_ref=halves.at[1 - k], dst_ref=half_in, send_sem=vv_send.at[0], recv_sem=vv_recv.at[0],
        device_id=(b, near[1]), device_id_type=MESH,
    )
    swap.start()
    pl.semaphore_wait(known.at[1], 3)
    swap.wait()
    half_in[...] += halves[k]

    here = 2 * h + l
    offsets = [(dx, dz, dy) for dx in range(RING) for dz in range(RING) for dy in range(RING) if dx or dz or dy]
    offsets.sort(key=lambda o: -sum(min(d, RING - d) for d in o))
    moved = {d: (lax.rem(cx + d, RING), lax.rem(cz + d, RING), lax.rem(here + d, RING)) for d in range(RING)}
    for n, (dx, dz, dy) in enumerate(offsets):
        tx, tz, ty = moved[dx][0], moved[dz][1], moved[dy][2]
        column = tx * RING + tz
        pltpu.make_async_remote_copy(
            src_ref=half_in.at[column * RING + ty], dst_ref=parts.at[n], send_sem=vv_send.at[1], recv_sem=vv_recv.at[1],
            device_id=(2 * column + ty // 2, 2 * lax.rem(ty, 2) + k), device_id_type=MESH,
        ).start()
    for n in (3, 2, 1):
        to_gamma(turns - n)
    everything = pltpu.make_async_remote_copy(
        src_ref=parts, dst_ref=parts, send_sem=vv_send.at[1], recv_sem=vv_recv.at[1],
        device_id=(b, near[1]), device_id_type=MESH,
    )
    everything.wait_recv()
    total = (half_in[(cx * RING + cz) * RING + here] + jnp.sum(parts[...], axis=0)) * scale
    vv_ref[:, 0:256] = total[0:4]
    vv_ref[:, 256:512] = total[4:8]
    everything.wait_send()

    for n in range(2):
        handed_back(n, "wait")
    for side in (0, 1):

        @pl.when(h == side)
        def _():
            for n in range(sends[side]):
                pltpu.make_async_remote_copy(
                    src_ref=x_ref.at[0], dst_ref=raw.at[0, 0], send_sem=send_sem.at[n], recv_sem=recv_sem.at[0, 0, 0],
                    device_id=(b, near[1]), device_id_type=MESH,
                ).wait_send()


def per_device(blocks, quarters, bints, occ_energy, vir_energy):
    rows, size, piece = bints.shape
    naux = piece * quarters
    pair_rows = rows // quarters
    f32, bf16 = jnp.float32, jnp.bfloat16
    scale = 1.0 / float(pair_rows * blocks * quarters * CYCLE * pair_rows)
    dma = pltpu.SemaphoreType.DMA
    chips = size // 8
    return pl.pallas_call(
        functools.partial(kernel, blocks, scale),
        out_shape=(
            jax.ShapeDtypeStruct((pair_rows, size, naux), f32),
            jax.ShapeDtypeStruct((size // (blocks * quarters), size), f32),
        ),
        in_specs=[
            pl.BlockSpec(memory_space=pltpu.HBM),
            pl.BlockSpec(memory_space=pltpu.SMEM),
            pl.BlockSpec(memory_space=pltpu.VMEM),
        ],
        out_specs=(pl.BlockSpec(memory_space=pltpu.VMEM), pl.BlockSpec(memory_space=pltpu.VMEM)),
        scratch_shapes=[
            pltpu.VMEM((3 * pair_rows, naux, size), bf16),
            pltpu.VMEM((pair_rows, 3, piece, size), bf16),
            pltpu.VMEM((2, piece, size), bf16),
            pltpu.VMEM((2, 2, piece, size), bf16),
            pltpu.VMEM((pair_rows, size, naux), bf16),
            pltpu.VMEM((size, size), f32),
            pltpu.VMEM((pair_rows, size, size), f32),
            pltpu.VMEM((pair_rows, size, size), bf16),
            pltpu.VMEM((3, pair_rows, size, size), bf16),
            pltpu.VMEM((size, 128), f32),
            pltpu.VMEM((2, chips, 8, 256), f32),
            pltpu.VMEM((chips, 8, 256), f32),
            pltpu.VMEM((chips - 1, 8, 256), f32),
            dma((2,)),
            dma((40,)),
            dma((3, 2, 4)),
            dma((2, 3)),
            dma((2,)),
            dma((2, 2)),
            dma((2, 2)),
            dma((2,)),
            dma((2,)),
            pltpu.SemaphoreType.REGULAR((2,)),
        ],
        compiler_params=pltpu.CompilerParams(
            collective_id=0, has_side_effects=True, vmem_limit_bytes=40 * 2**20
        ),
        name="pair_densities",
    )(pltpu.with_memory_space_constraint(jnp.swapaxes(bints, 1, 2), pltpu.HBM), pltpu.with_memory_space_constraint(occ_energy, pltpu.HBM), pltpu.with_memory_space_constraint(vir_energy.reshape(1, size), pltpu.HBM))


def solution(mesh):
    return jax.shard_map(
        functools.partial(per_device, mesh.shape["blk"], mesh.shape["quarter"]),
        mesh=mesh,
        in_specs=(P("blk", None, "quarter"), P(), P()),
        out_specs=(P(("blk", "quarter"), None, None), P(("blk", "quarter"), None)),
        check_vma=False,
    )
```

```python
import functools

import jax
import jax.numpy as jnp
from jax import lax
from jax.experimental import pallas as pl
from jax.experimental.pallas import tpu as pltpu
from jax.sharding import PartitionSpec as P

CYCLE = 3
RING = 4
MESH = pl.DeviceIdType.MESH
NT = (((1,), (1,)), ((), ()))
X, Y, Z = 0, 1, 2


def kernel(
    blocks,
    scale,
    x_ref,
    occ_ref,
    vir_ref,
    acc,
    vv_ref,
    held,
    raw,
    relay,
    back,
    own_t,
    vv,
    amp,
    amp_b,
    tilde,
    vir_col,
    halves,
    half_in,
    parts,
    local_sem,
    send_sem,
    recv_sem,
    raw_sem,
    relay_sem,
    back_send,
    back_recv,
    vv_send,
    vv_recv,
    known,
):
    piece = x_ref.shape[1]
    b, q = lax.axis_index("blk"), lax.axis_index("quarter")
    col, h, l, k = b // 2, lax.rem(b, 2), q // 2, lax.rem(q, 2)
    cx, cz = col // RING, lax.rem(col, RING)
    near = [q, 2 * l + 1 - k, 2 * (1 - l) + k, 2 * (1 - l) + 1 - k]
    ahead, behind = lax.rem(b + 2, blocks), lax.rem(b + blocks - 2, blocks)
    across = 2 * col + 1 - h

    def along_z(step):
        return 2 * (cx * RING + lax.rem(cz + step, RING)) + h

    def along_x(step):
        return 2 * (lax.rem(cx + step, RING) * RING + cz) + h

    barrier = pltpu.get_barrier_semaphore()
    peers = [(b, near[d]) for d in (1, 2, 3)] + [(across, near[d]) for d in range(4)] + [(ahead, q), (behind, q)]
    peers += [(along_z(s), q) for s in (1, 2, 3)] + [(along_x(s), q) for s in (1, 2, 3)]
    for peer in peers:
        pl.semaphore_signal(barrier, inc=1, device_id=peer, device_id_type=MESH)

    def slot(which, j, p):
        return held.at[which * 2 + j, pl.ds(pl.multiple_of(p * piece, piece), piece), :]

    sends = {0: 0, 1: 0}

    def send(side, src, dst, sem, device):
        n = sends[side]
        copy = pltpu.make_async_remote_copy(
            src_ref=src, dst_ref=dst, send_sem=send_sem.at[n], recv_sem=sem, device_id=device, device_id_type=MESH
        )
        copy.start()
        sends[side] = n + 1

    def to_slot(side, src, which, j, p, device):
        send(side, src, slot(which, j, p), recv_sem.at[which, j, p], device)

    def arrived(dst, sem):
        pltpu.make_async_remote_copy(
            src_ref=dst, dst_ref=dst, send_sem=send_sem.at[0], recv_sem=sem, device_id=(b, near[1]), device_id_type=MESH
        ).wait_recv()

    def slot_arrived(which, j, p):
        arrived(slot(which, j, p), recv_sem.at[which, j, p])

    def mine(r, j):
        return x_ref.at[2 * r + j]

    own_copies = [pltpu.make_async_copy(mine(q, j), slot(X, j, q), local_sem.at[j]) for j in range(2)]
    for copy in own_copies:
        copy.start()
    pl.semaphore_wait(barrier, len(peers))

    odd = lax.rem(cz, 2)
    halfway = jnp.where(odd == 1, along_z(2), along_z(3))

    def send_back(side, src, n):
        send(side, src, back.at[odd, n], back_recv.at[odd, n], (halfway, q))

    @pl.when(h == 0)
    def _():
        for d in (1, 2, 3):
            to_slot(0, mine(near[d], 0), X, 0, q, (b, near[d]))
        to_slot(0, mine(near[1], 1), X, 1, q, (b, near[1]))
        to_slot(0, mine(q, 0), Y, 0, q, (ahead, q))
        send_back(0, mine(q, 1), 0)
        for d in (2, 3):
            to_slot(0, mine(near[d], 0), Y, 0, q, (across, near[d]))
        for d in (2, 3):
            to_slot(0, mine(near[d], 1), X, 1, q, (b, near[d]))
        for d in (2, 3):
            to_slot(0, mine(near[d], 1), Y, 1, q, (across, near[d]))
        for j in range(2):
            for d in (0, 1):
                to_slot(0, mine(near[d], j), Y, j, q, (across, near[d]))

    @pl.when(h == 1)
    def _():
        for d in (2, 3):
            send(1, mine(near[d], 1), relay.at[d - 2], relay_sem.at[d - 2], (across, near[d]))
        for d in (1, 2, 3):
            to_slot(1, mine(near[d], 0), X, 0, q, (b, near[d]))
        to_slot(1, mine(near[1], 1), X, 1, q, (b, near[1]))
        to_slot(1, mine(q, 0), Z, 0, q, (ahead, q))
        send_back(1, mine(near[1], 0), 0)
        for d in (2, 3):
            send(1, mine(near[d], 0), raw.at[0, d - 1], raw_sem.at[0, d - 1], (ahead, q))
        to_slot(1, mine(q, 1), Z, 1, q, (ahead, q))
        send_back(1, mine(near[1], 1), 1)

    for s in (1, 2, 3):
        pl.semaphore_signal(known.at[0], inc=1, device_id=(along_z(s), q), device_id_type=MESH)
    acc[...] = jnp.zeros_like(acc)
    vv[...] = jnp.zeros_like(vv)
    vir_col[...] = jnp.transpose(jnp.broadcast_to(vir_ref[...], (128, vir_ref.shape[1])))

    def own_piece(j, d, sides=(0, 1)):
        slot_arrived(X, j, near[d])

        if 0 in sides:

            @pl.when(h == 0)
            def _():
                if (j, d) == (1, 1):
                    send_back(0, slot(X, j, near[d]), 1)
                else:
                    to_slot(0, slot(X, j, near[d]), Y, j, near[d], (ahead, q))

        if d > 1 and 1 in sides:

            @pl.when(h == 1)
            def _():
                to_slot(1, slot(X, j, near[d]), Z, j, near[d], (ahead, q))

    def passed_on(j, d):
        @pl.when(h == 1)
        def _():
            if d == 0:
                slot_arrived(Z, j, q)
                to_slot(1, slot(Z, j, q), Z, j, q, (across, q))
                if j == 0:
                    for own in (2, 3):
                        to_slot(1, mine(near[own], 1), X, 1, q, (b, near[own]))
                return
            src = raw.at[j, d - 1]
            arrived(src, raw_sem.at[j, d - 1])
            to_slot(1, src, Z, j, q, (across, near[d]))
            if d == 1:
                to_slot(1, src, Z, j, q, (b, near[d]))

    def relayed():
        @pl.when(h == 0)
        def _():
            for d in (2, 3):
                arrived(relay.at[d - 2], relay_sem.at[d - 2])
                to_slot(0, relay.at[d - 2], Z, 1, near[d], (ahead, q))

    def handed_back(n, act):
        for e in (0, 1):
            source = cx * RING + lax.rem(cz + 1 + e, RING)
            device = (lax.rem(2 * source + 2 + h, blocks), q)
            copy = functools.partial(
                pltpu.make_async_remote_copy,
                src_ref=back.at[e, n], send_sem=back_send.at[e, n], device_id=device, device_id_type=MESH,
            )
            to_raw = copy(dst_ref=raw.at[n, 0], recv_sem=raw_sem.at[n, 0])
            if act == "wait":

                @pl.when(odd == 1)
                def _():
                    to_raw.wait_send()

                continue

            @pl.when(odd == 1)
            def _():
                arrived(back.at[e, n], back_recv.at[e, n])

            @pl.when(jnp.logical_and(odd == 1, h == 1))
            def _():
                to_raw.start()

            p = near[n]

            @pl.when(jnp.logical_and(odd == 1, h == 0))
            def _():
                copy(dst_ref=slot(Y, 1, p), recv_sem=recv_sem.at[Y, 1, p]).start()

    def last_piece(j):
        @pl.when(h == 0)
        def _():
            slot_arrived(Z, j, q)

        for d in (1, 2, 3):
            slot_arrived(Z, j, near[d])

    def turned(i):
        for n in range(held.shape[1] // 256):
            rows = pl.ds(n * 256, 256)
            own_t[i, :, rows] = jnp.transpose(held[2 * X + i, rows, :])

    def before(turn):
        @pl.when(turn == 1)
        def _():
            passed_on(0, 1)

        @pl.when(turn == 2)
        def _():
            for p in range(4):
                slot_arrived(Y, 0, p)

        @pl.when(turn == 3)
        def _():
            passed_on(1, 1)
            last_piece(0)

        @pl.when(turn == 4)
        def _():
            for p in range(4):
                slot_arrived(Y, 1, p)

        @pl.when(turn == 5)
        def _():
            last_piece(1)

    for copy in own_copies:
        copy.wait()
    own_piece(0, 1)
    own_piece(1, 1)
    own_piece(0, 2)
    passed_on(0, 0)
    own_piece(0, 3)
    passed_on(0, 2)
    pl.semaphore_wait(known.at[0], 3)
    for s in (1, 2, 3):
        pl.semaphore_signal(known.at[1], inc=1, device_id=(along_x(s), q), device_id_type=MESH)
    turned(0)
    passed_on(0, 3)

    @pl.when(h == 0)
    def _():
        own_piece(1, 2, (0,))
        handed_back(0, "start")
        own_piece(1, 3, (0,))

    relayed()

    @pl.when(h == 0)
    def _():
        handed_back(1, "start")

    @pl.when(h == 1)
    def _():
        handed_back(0, "start")
        own_piece(1, 2, (1,))

    passed_on(1, 0)

    @pl.when(h == 1)
    def _():
        handed_back(1, "start")
        own_piece(1, 3, (1,))

    turned(1)

    size = vir_ref.shape[1]

    turns, late = 2 * CYCLE, tilde.shape[0]
    rows_both = 2 * size

    def place(turn):
        which = jnp.where(turn < 2, X, Y + lax.rem(turn, 2))
        return which, jnp.where(turn < 2, turn, (turn - 2) // 2)

    def to_gamma(turn):
        which, j = place(turn)
        other = held.at[which * 2 + j]
        both = tilde[lax.rem(turn, late)].reshape(rows_both, size)
        for n in range(held.shape[1] // 256):
            rows = pl.ds(n * 256, 256)
            terms = lax.dot_general(both, other[rows, :], NT, preferred_element_type=jnp.float32)
            acc[:, :, rows] += terms.reshape(2, size, 256)

    def pairs(turn, carry):
        before(turn)
        which, j = place(turn)
        slot_out = lax.rem(turn, late)
        behind_by = jnp.where(which == X, 0, jnp.where(which == Y, 2 - h, 1 + h))
        partner = lax.rem(b - behind_by + blocks, blocks)
        e_j = occ_ref[(partner * 4 + q) * 2 + j]
        other = held.at[which * 2 + j]
        for n in range(size // 256):
            cols = pl.ds(n * 256, 256)
            pairint = jnp.dot(own_t[...].reshape(rows_both, -1), other[:, cols], preferred_element_type=jnp.float32)
            for i in range(2):
                e_i = occ_ref[(b * 4 + q) * 2 + i]
                for m in range(2):
                    lanes = pl.ds(n * 256 + m * 128, 128)
                    denom = vir_col[...] + vir_ref[:, lanes] - e_i - e_j
                    ratio = pairint[i * size : (i + 1) * size, m * 128 : (m + 1) * 128] / denom
                    amp[i, :, lanes] = ratio
                    amp_b[i, :, lanes] = ratio.astype(jnp.bfloat16)
        for i in range(2):
            for n in range(size // 128):
                rows = pl.ds(n * 128, 128)
                turned_back = jnp.transpose(amp[i, :, rows])
                tilde[slot_out, i, rows, :] = (2.0 * amp[i, rows, :] - turned_back).astype(jnp.bfloat16)
            vv[...] += lax.dot_general(amp_b[i], tilde[slot_out, i], NT, preferred_element_type=jnp.float32)

        @pl.when(turn < turns - late)
        def _():
            to_gamma(turn)

        return carry

    lax.fori_loop(0, turns, pairs, 0)

    low = lax.broadcasted_iota(jnp.int32, (8, 256), 0) < 4
    for chip in range(size // 8):
        rows = pl.ds(chip * 8, 8)
        left, right = vv[rows, 0:256], vv[rows, 256:512]
        halves[0, chip] = jnp.where(low, left, pltpu.roll(right, 4, 0))
        halves[1, chip] = jnp.where(low, pltpu.roll(left, 4, 0), right)

    swap = pltpu.make_async_remote_copy(
        src_ref=halves.at[1 - k], dst_ref=half_in, send_sem=vv_send.at[0], recv_sem=vv_recv.at[0],
        device_id=(b, near[1]), device_id_type=MESH,
    )
    swap.start()
    pl.semaphore_wait(known.at[1], 3)
    swap.wait()
    half_in[...] += halves[k]

    here = 2 * h + l
    offsets = [(dx, dz, dy) for dx in range(RING) for dz in range(RING) for dy in range(RING) if dx or dz or dy]
    offsets.sort(key=lambda o: -sum(min(d, RING - d) for d in o))
    moved = {d: (lax.rem(cx + d, RING), lax.rem(cz + d, RING), lax.rem(here + d, RING)) for d in range(RING)}
    for n, (dx, dz, dy) in enumerate(offsets):
        tx, tz, ty = moved[dx][0], moved[dz][1], moved[dy][2]
        column = tx * RING + tz
        pltpu.make_async_remote_copy(
            src_ref=half_in.at[column * RING + ty], dst_ref=parts.at[n], send_sem=vv_send.at[1], recv_sem=vv_recv.at[1],
            device_id=(2 * column + ty // 2, 2 * lax.rem(ty, 2) + k), device_id_type=MESH,
        ).start()
    for n in (3, 2, 1):
        to_gamma(turns - n)
    everything = pltpu.make_async_remote_copy(
        src_ref=parts, dst_ref=parts, send_sem=vv_send.at[1], recv_sem=vv_recv.at[1],
        device_id=(b, near[1]), device_id_type=MESH,
    )
    everything.wait_recv()
    total = (half_in[(cx * RING + cz) * RING + here] + jnp.sum(parts[...], axis=0)) * scale
    vv_ref[:, 0:256] = total[0:4]
    vv_ref[:, 256:512] = total[4:8]
    everything.wait_send()

    for n in range(2):
        handed_back(n, "wait")
    for side in (0, 1):

        @pl.when(h == side)
        def _():
            for n in range(sends[side]):
                pltpu.make_async_remote_copy(
                    src_ref=x_ref.at[0], dst_ref=raw.at[0, 0], send_sem=send_sem.at[n], recv_sem=recv_sem.at[0, 0, 0],
                    device_id=(b, near[1]), device_id_type=MESH,
                ).wait_send()


def put_out(gamma_ref, rows_ref, gamma_out, rows_out, sems):
    copies = [pltpu.make_async_copy(rows_ref, rows_out, sems.at[0])]
    cut = gamma_ref.shape[1] // 4
    for i in range(gamma_ref.shape[0]):
        for n in range(4):
            part = pl.ds(n * cut, cut)
            copies.append(pltpu.make_async_copy(gamma_ref.at[i, part], gamma_out.at[i, part], sems.at[1 + 4 * i + n]))
    for copy in copies:
        copy.start()
    for copy in copies:
        copy.wait()


def per_device(blocks, quarters, bints, occ_energy, vir_energy):
    rows, size, piece = bints.shape
    naux = piece * quarters
    pair_rows = rows // quarters
    f32, bf16 = jnp.float32, jnp.bfloat16
    scale = 1.0 / float(pair_rows * blocks * quarters * CYCLE * pair_rows)
    dma = pltpu.SemaphoreType.DMA
    chips = size // 8
    gamma, rows_own = pl.pallas_call(
        functools.partial(kernel, blocks, scale),
        out_shape=(
            jax.ShapeDtypeStruct((pair_rows, size, naux), f32),
            jax.ShapeDtypeStruct((size // (blocks * quarters), size), f32),
        ),
        in_specs=[
            pl.BlockSpec(memory_space=pltpu.HBM),
            pl.BlockSpec(memory_space=pltpu.SMEM),
            pl.BlockSpec(memory_space=pltpu.VMEM),
        ],
        out_specs=(pl.BlockSpec(memory_space=pltpu.VMEM), pl.BlockSpec(memory_space=pltpu.VMEM)),
        scratch_shapes=[
            pltpu.VMEM((3 * pair_rows, naux, size), bf16),
            pltpu.VMEM((pair_rows, 3, piece, size), bf16),
            pltpu.VMEM((2, piece, size), bf16),
            pltpu.VMEM((2, 2, piece, size), bf16),
            pltpu.VMEM((pair_rows, size, naux), bf16),
            pltpu.VMEM((size, size), f32),
            pltpu.VMEM((pair_rows, size, size), f32),
            pltpu.VMEM((pair_rows, size, size), bf16),
            pltpu.VMEM((3, pair_rows, size, size), bf16),
            pltpu.VMEM((size, 128), f32),
            pltpu.VMEM((2, chips, 8, 256), f32),
            pltpu.VMEM((chips, 8, 256), f32),
            pltpu.VMEM((chips - 1, 8, 256), f32),
            dma((2,)),
            dma((40,)),
            dma((3, 2, 4)),
            dma((2, 3)),
            dma((2,)),
            dma((2, 2)),
            dma((2, 2)),
            dma((2,)),
            dma((2,)),
            pltpu.SemaphoreType.REGULAR((2,)),
        ],
        compiler_params=pltpu.CompilerParams(
            collective_id=0, has_side_effects=True, vmem_limit_bytes=40 * 2**20
        ),
        name="pair_densities",
    )(pltpu.with_memory_space_constraint(jnp.swapaxes(bints, 1, 2), pltpu.HBM), pltpu.with_memory_space_constraint(occ_energy, pltpu.HBM), pltpu.with_memory_space_constraint(vir_energy.reshape(1, size), pltpu.HBM))

    return pl.pallas_call(
        put_out,
        out_shape=(jax.ShapeDtypeStruct(gamma.shape, f32), jax.ShapeDtypeStruct(rows_own.shape, f32)),
        in_specs=[pl.BlockSpec(memory_space=pl.ANY)] * 2,
        out_specs=(pl.BlockSpec(memory_space=pl.ANY),) * 2,
        scratch_shapes=[dma((1 + 4 * pair_rows,))],
        compiler_params=pltpu.CompilerParams(vmem_limit_bytes=2**20),
        name="put_out",
    )(gamma, rows_own)


def solution(mesh):
    return jax.shard_map(
        functools.partial(per_device, mesh.shape["blk"], mesh.shape["quarter"]),
        mesh=mesh,
        in_specs=(P("blk", None, "quarter"), P(), P()),
        out_specs=(P(("blk", "quarter"), None, None), P(("blk", "quarter"), None)),
        check_vma=False,
    )
```

```python
import functools

import jax
import jax.numpy as jnp
from jax import lax
from jax.experimental import pallas as pl
from jax.experimental.pallas import tpu as pltpu
from jax.sharding import PartitionSpec as P

CYCLE = 3
RING = 4
MESH = pl.DeviceIdType.MESH
NT = (((1,), (1,)), ((), ()))
X, Y, Z = 0, 1, 2


def kernel(
    blocks,
    scale,
    x_ref,
    occ_ref,
    vir_ref,
    acc,
    vv_ref,
    held,
    raw,
    relay,
    back,
    own_t,
    vv,
    amp,
    amp_b,
    tilde,
    vir_col,
    halves,
    half_in,
    parts,
    local_sem,
    send_sem,
    recv_sem,
    raw_sem,
    relay_sem,
    back_send,
    back_recv,
    vv_send,
    vv_recv,
    known,
):
    piece = x_ref.shape[1]
    b, q = lax.axis_index("blk"), lax.axis_index("quarter")
    col, h, l, k = b // 2, lax.rem(b, 2), q // 2, lax.rem(q, 2)
    cx, cz = col // RING, lax.rem(col, RING)
    near = [q, 2 * l + 1 - k, 2 * (1 - l) + k, 2 * (1 - l) + 1 - k]
    ahead, behind = lax.rem(b + 2, blocks), lax.rem(b + blocks - 2, blocks)
    across = 2 * col + 1 - h

    def along_z(step):
        return 2 * (cx * RING + lax.rem(cz + step, RING)) + h

    def along_x(step):
        return 2 * (lax.rem(cx + step, RING) * RING + cz) + h

    barrier = pltpu.get_barrier_semaphore()
    peers = [(b, near[d]) for d in (1, 2, 3)] + [(across, near[d]) for d in range(4)] + [(ahead, q), (behind, q)]
    peers += [(along_z(s), q) for s in (1, 2, 3)] + [(along_x(s), q) for s in (1, 2, 3)]
    for peer in peers:
        pl.semaphore_signal(barrier, inc=1, device_id=peer, device_id_type=MESH)

    def slot(which, j, p):
        return held.at[which * 2 + j, pl.ds(pl.multiple_of(p * piece, piece), piece), :]

    sends = {0: 0, 1: 0}

    def send(side, src, dst, sem, device):
        n = sends[side]
        copy = pltpu.make_async_remote_copy(
            src_ref=src, dst_ref=dst, send_sem=send_sem.at[n], recv_sem=sem, device_id=device, device_id_type=MESH
        )
        copy.start()
        sends[side] = n + 1

    def to_slot(side, src, which, j, p, device):
        send(side, src, slot(which, j, p), recv_sem.at[which, j, p], device)

    def arrived(dst, sem):
        pltpu.make_async_remote_copy(
            src_ref=dst, dst_ref=dst, send_sem=send_sem.at[0], recv_sem=sem, device_id=(b, near[1]), device_id_type=MESH
        ).wait_recv()

    def slot_arrived(which, j, p):
        arrived(slot(which, j, p), recv_sem.at[which, j, p])

    def mine(r, j):
        return x_ref.at[2 * r + j]

    own_copies = [pltpu.make_async_copy(mine(q, j), slot(X, j, q), local_sem.at[j]) for j in range(2)]
    for copy in own_copies:
        copy.start()
    pl.semaphore_wait(barrier, len(peers))

    odd = lax.rem(cz, 2)
    halfway = jnp.where(odd == 1, along_z(2), along_z(3))

    def send_back(side, src, n):
        send(side, src, back.at[odd, n], back_recv.at[odd, n], (halfway, q))

    @pl.when(h == 0)
    def _():
        for d in (1, 2, 3):
            to_slot(0, mine(near[d], 0), X, 0, q, (b, near[d]))
        to_slot(0, mine(near[1], 1), X, 1, q, (b, near[1]))
        to_slot(0, mine(q, 0), Y, 0, q, (ahead, q))
        send_back(0, mine(q, 1), 0)
        for d in (2, 3):
            to_slot(0, mine(near[d], 0), Y, 0, q, (across, near[d]))
        for d in (2, 3):
            to_slot(0, mine(near[d], 1), X, 1, q, (b, near[d]))
        for d in (2, 3):
            to_slot(0, mine(near[d], 1), Y, 1, q, (across, near[d]))
        for j in range(2):
            for d in (0, 1):
                to_slot(0, mine(near[d], j), Y, j, q, (across, near[d]))

    @pl.when(h == 1)
    def _():
        for d in (2, 3):
            send(1, mine(near[d], 1), relay.at[d - 2], relay_sem.at[d - 2], (across, near[d]))
        for d in (1, 2, 3):
            to_slot(1, mine(near[d], 0), X, 0, q, (b, near[d]))
        to_slot(1, mine(near[1], 1), X, 1, q, (b, near[1]))
        to_slot(1, mine(q, 0), Z, 0, q, (ahead, q))
        send_back(1, mine(near[1], 0), 0)
        for d in (2, 3):
            send(1, mine(near[d], 0), raw.at[0, d - 1], raw_sem.at[0, d - 1], (ahead, q))
        to_slot(1, mine(q, 1), Z, 1, q, (ahead, q))
        send_back(1, mine(near[1], 1), 1)

    for s in (1, 2, 3):
        pl.semaphore_signal(known.at[0], inc=1, device_id=(along_z(s), q), device_id_type=MESH)
    acc[...] = jnp.zeros_like(acc)
    vv[...] = jnp.zeros_like(vv)
    vir_col[...] = jnp.transpose(jnp.broadcast_to(vir_ref[...], (128, vir_ref.shape[1])))

    def own_piece(j, d, sides=(0, 1)):
        slot_arrived(X, j, near[d])

        if 0 in sides:

            @pl.when(h == 0)
            def _():
                if (j, d) == (1, 1):
                    send_back(0, slot(X, j, near[d]), 1)
                else:
                    to_slot(0, slot(X, j, near[d]), Y, j, near[d], (ahead, q))

        if d > 1 and 1 in sides:

            @pl.when(h == 1)
            def _():
                to_slot(1, slot(X, j, near[d]), Z, j, near[d], (ahead, q))

    def passed_on(j, d):
        @pl.when(h == 1)
        def _():
            if d == 0:
                slot_arrived(Z, j, q)
                to_slot(1, slot(Z, j, q), Z, j, q, (across, q))
                if j == 0:
                    for own in (2, 3):
                        to_slot(1, mine(near[own], 1), X, 1, q, (b, near[own]))
                return
            src = raw.at[j, d - 1]
            arrived(src, raw_sem.at[j, d - 1])
            to_slot(1, src, Z, j, q, (across, near[d]))
            if d == 1:
                to_slot(1, src, Z, j, q, (b, near[d]))

    def relayed():
        @pl.when(h == 0)
        def _():
            for d in (2, 3):
                arrived(relay.at[d - 2], relay_sem.at[d - 2])
                to_slot(0, relay.at[d - 2], Z, 1, near[d], (ahead, q))

    def handed_back(n, act):
        for e in (0, 1):
            source = cx * RING + lax.rem(cz + 1 + e, RING)
            device = (lax.rem(2 * source + 2 + h, blocks), q)
            copy = functools.partial(
                pltpu.make_async_remote_copy,
                src_ref=back.at[e, n], send_sem=back_send.at[e, n], device_id=device, device_id_type=MESH,
            )
            to_raw = copy(dst_ref=raw.at[n, 0], recv_sem=raw_sem.at[n, 0])
            if act == "wait":

                @pl.when(odd == 1)
                def _():
                    to_raw.wait_send()

                continue

            @pl.when(odd == 1)
            def _():
                arrived(back.at[e, n], back_recv.at[e, n])

            @pl.when(jnp.logical_and(odd == 1, h == 1))
            def _():
                to_raw.start()

            p = near[n]

            @pl.when(jnp.logical_and(odd == 1, h == 0))
            def _():
                copy(dst_ref=slot(Y, 1, p), recv_sem=recv_sem.at[Y, 1, p]).start()

    def last_piece(j):
        @pl.when(h == 0)
        def _():
            slot_arrived(Z, j, q)

        for d in (1, 2, 3):
            slot_arrived(Z, j, near[d])

    def turned(i):
        for n in range(held.shape[1] // 256):
            rows = pl.ds(n * 256, 256)
            own_t[i, :, rows] = jnp.transpose(held[2 * X + i, rows, :])

    def before(turn):
        @pl.when(turn == 1)
        def _():
            passed_on(0, 1)

        @pl.when(turn == 2)
        def _():
            for p in range(4):
                slot_arrived(Y, 0, p)

        @pl.when(turn == 3)
        def _():
            passed_on(1, 1)
            last_piece(0)

        @pl.when(turn == 4)
        def _():
            for p in range(4):
                slot_arrived(Y, 1, p)

        @pl.when(turn == 5)
        def _():
            last_piece(1)

    for copy in own_copies:
        copy.wait()
    own_piece(0, 1)
    own_piece(1, 1)
    own_piece(0, 2)
    passed_on(0, 0)
    own_piece(0, 3)
    passed_on(0, 2)
    pl.semaphore_wait(known.at[0], 3)
    for s in (1, 2, 3):
        pl.semaphore_signal(known.at[1], inc=1, device_id=(along_x(s), q), device_id_type=MESH)
    turned(0)
    passed_on(0, 3)

    @pl.when(h == 0)
    def _():
        own_piece(1, 2, (0,))
        handed_back(0, "start")
        own_piece(1, 3, (0,))

    relayed()

    @pl.when(h == 0)
    def _():
        handed_back(1, "start")

    @pl.when(h == 1)
    def _():
        handed_back(0, "start")
        own_piece(1, 2, (1,))

    passed_on(1, 0)

    @pl.when(h == 1)
    def _():
        handed_back(1, "start")
        own_piece(1, 3, (1,))

    turned(1)

    size = vir_ref.shape[1]

    turns, late = 2 * CYCLE, tilde.shape[0]
    rows_both = 2 * size

    def place(turn):
        which = jnp.where(turn < 2, X, Y + lax.rem(turn, 2))
        return which, jnp.where(turn < 2, turn, (turn - 2) // 2)

    def to_gamma(turn):
        which, j = place(turn)
        other = held.at[which * 2 + j]
        both = tilde[lax.rem(turn, late)].reshape(rows_both, size)
        for n in range(held.shape[1] // 256):
            rows = pl.ds(n * 256, 256)
            terms = lax.dot_general(both, other[rows, :], NT, preferred_element_type=jnp.float32)
            acc[:, :, rows] += terms.reshape(2, size, 256)

    def pairs(turn, carry):
        before(turn)
        which, j = place(turn)
        slot_out = lax.rem(turn, late)
        behind_by = jnp.where(which == X, 0, jnp.where(which == Y, 2 - h, 1 + h))
        partner = lax.rem(b - behind_by + blocks, blocks)
        e_j = occ_ref[(partner * 4 + q) * 2 + j]
        other = held.at[which * 2 + j]
        for n in range(size // 256):
            cols = pl.ds(n * 256, 256)
            pairint = jnp.dot(own_t[...].reshape(rows_both, -1), other[:, cols], preferred_element_type=jnp.float32)
            for i in range(2):
                e_i = occ_ref[(b * 4 + q) * 2 + i]
                for m in range(2):
                    lanes = pl.ds(n * 256 + m * 128, 128)
                    denom = vir_col[...] + vir_ref[:, lanes] - e_i - e_j
                    ratio = pairint[i * size : (i + 1) * size, m * 128 : (m + 1) * 128] / denom
                    amp[i, :, lanes] = ratio
                    amp_b[i, :, lanes] = ratio.astype(jnp.bfloat16)
        for i in range(2):
            for n in range(size // 128):
                rows = pl.ds(n * 128, 128)
                turned_back = jnp.transpose(amp[i, :, rows])
                tilde[slot_out, i, rows, :] = (2.0 * amp[i, rows, :] - turned_back).astype(jnp.bfloat16)
            vv[...] += lax.dot_general(amp_b[i], tilde[slot_out, i], NT, preferred_element_type=jnp.float32)

        @pl.when(turn < turns - late)
        def _():
            to_gamma(turn)

        return carry

    lax.fori_loop(0, turns, pairs, 0)

    low = lax.broadcasted_iota(jnp.int32, (8, 256), 0) < 4
    swaps = []
    for half in range(2):
        part = pl.ds(half * (size // 16), size // 16)
        for chip in range(half * (size // 16), (half + 1) * (size // 16)):
            rows = pl.ds(chip * 8, 8)
            left, right = vv[rows, 0:256], vv[rows, 256:512]
            halves[0, chip] = jnp.where(low, left, pltpu.roll(right, 4, 0))
            halves[1, chip] = jnp.where(low, pltpu.roll(left, 4, 0), right)
        swap = pltpu.make_async_remote_copy(
            src_ref=halves.at[1 - k, part], dst_ref=half_in.at[part],
            send_sem=vv_send.at[2 * half], recv_sem=vv_recv.at[2 * half],
            device_id=(b, near[1]), device_id_type=MESH,
        )
        swap.start()
        swaps.append((swap, part))
    pl.semaphore_wait(known.at[1], 3)
    for swap, part in swaps:
        swap.wait()
        half_in[part] += halves[k, part]

    here = 2 * h + l
    offsets = [(dx, dz, dy) for dx in range(RING) for dz in range(RING) for dy in range(RING) if dx or dz or dy]
    offsets.sort(key=lambda o: -sum(min(d, RING - d) for d in o))
    moved = {d: (lax.rem(cx + d, RING), lax.rem(cz + d, RING), lax.rem(here + d, RING)) for d in range(RING)}
    for n, (dx, dz, dy) in enumerate(offsets):
        tx, tz, ty = moved[dx][0], moved[dz][1], moved[dy][2]
        column = tx * RING + tz
        pltpu.make_async_remote_copy(
            src_ref=half_in.at[column * RING + ty], dst_ref=parts.at[n], send_sem=vv_send.at[1], recv_sem=vv_recv.at[1],
            device_id=(2 * column + ty // 2, 2 * lax.rem(ty, 2) + k), device_id_type=MESH,
        ).start()
    for n in (3, 2, 1):
        to_gamma(turns - n)
    everything = pltpu.make_async_remote_copy(
        src_ref=parts, dst_ref=parts, send_sem=vv_send.at[1], recv_sem=vv_recv.at[1],
        device_id=(b, near[1]), device_id_type=MESH,
    )
    everything.wait_recv()
    total = (half_in[(cx * RING + cz) * RING + here] + jnp.sum(parts[...], axis=0)) * scale
    vv_ref[:, 0:256] = total[0:4]
    vv_ref[:, 256:512] = total[4:8]
    everything.wait_send()

    for n in range(2):
        handed_back(n, "wait")
    for side in (0, 1):

        @pl.when(h == side)
        def _():
            for n in range(sends[side]):
                pltpu.make_async_remote_copy(
                    src_ref=x_ref.at[0], dst_ref=raw.at[0, 0], send_sem=send_sem.at[n], recv_sem=recv_sem.at[0, 0, 0],
                    device_id=(b, near[1]), device_id_type=MESH,
                ).wait_send()


def put_out(gamma_ref, rows_ref, gamma_out, rows_out, sems):
    copies = [pltpu.make_async_copy(rows_ref, rows_out, sems.at[0])]
    cut = gamma_ref.shape[1] // 4
    for i in range(gamma_ref.shape[0]):
        for n in range(4):
            part = pl.ds(n * cut, cut)
            copies.append(pltpu.make_async_copy(gamma_ref.at[i, part], gamma_out.at[i, part], sems.at[1 + 4 * i + n]))
    for copy in copies:
        copy.start()
    for copy in copies:
        copy.wait()


def per_device(blocks, quarters, bints, occ_energy, vir_energy):
    rows, size, piece = bints.shape
    naux = piece * quarters
    pair_rows = rows // quarters
    f32, bf16 = jnp.float32, jnp.bfloat16
    scale = 1.0 / float(pair_rows * blocks * quarters * CYCLE * pair_rows)
    dma = pltpu.SemaphoreType.DMA
    chips = size // 8
    gamma, rows_own = pl.pallas_call(
        functools.partial(kernel, blocks, scale),
        out_shape=(
            jax.ShapeDtypeStruct((pair_rows, size, naux), f32),
            jax.ShapeDtypeStruct((size // (blocks * quarters), size), f32),
        ),
        in_specs=[
            pl.BlockSpec(memory_space=pltpu.HBM),
            pl.BlockSpec(memory_space=pltpu.SMEM),
            pl.BlockSpec(memory_space=pltpu.VMEM),
        ],
        out_specs=(pl.BlockSpec(memory_space=pltpu.VMEM), pl.BlockSpec(memory_space=pltpu.VMEM)),
        scratch_shapes=[
            pltpu.VMEM((3 * pair_rows, naux, size), bf16),
            pltpu.VMEM((pair_rows, 3, piece, size), bf16),
            pltpu.VMEM((2, piece, size), bf16),
            pltpu.VMEM((2, 2, piece, size), bf16),
            pltpu.VMEM((pair_rows, size, naux), bf16),
            pltpu.VMEM((size, size), f32),
            pltpu.VMEM((pair_rows, size, size), f32),
            pltpu.VMEM((pair_rows, size, size), bf16),
            pltpu.VMEM((3, pair_rows, size, size), bf16),
            pltpu.VMEM((size, 128), f32),
            pltpu.VMEM((2, chips, 8, 256), f32),
            pltpu.VMEM((chips, 8, 256), f32),
            pltpu.VMEM((chips - 1, 8, 256), f32),
            dma((2,)),
            dma((40,)),
            dma((3, 2, 4)),
            dma((2, 3)),
            dma((2,)),
            dma((2, 2)),
            dma((2, 2)),
            dma((3,)),
            dma((3,)),
            pltpu.SemaphoreType.REGULAR((2,)),
        ],
        compiler_params=pltpu.CompilerParams(
            collective_id=0, has_side_effects=True, vmem_limit_bytes=40 * 2**20
        ),
        name="pair_densities",
    )(pltpu.with_memory_space_constraint(jnp.swapaxes(bints, 1, 2), pltpu.HBM), pltpu.with_memory_space_constraint(occ_energy, pltpu.HBM), pltpu.with_memory_space_constraint(vir_energy.reshape(1, size), pltpu.HBM))

    return pl.pallas_call(
        put_out,
        out_shape=(jax.ShapeDtypeStruct(gamma.shape, f32), jax.ShapeDtypeStruct(rows_own.shape, f32)),
        in_specs=[pl.BlockSpec(memory_space=pl.ANY)] * 2,
        out_specs=(pl.BlockSpec(memory_space=pl.ANY),) * 2,
        scratch_shapes=[dma((1 + 4 * pair_rows,))],
        compiler_params=pltpu.CompilerParams(vmem_limit_bytes=2**20),
        name="put_out",
    )(gamma, rows_own)


def solution(mesh):
    return jax.shard_map(
        functools.partial(per_device, mesh.shape["blk"], mesh.shape["quarter"]),
        mesh=mesh,
        in_specs=(P("blk", None, "quarter"), P(), P()),
        out_specs=(P(("blk", "quarter"), None, None), P(("blk", "quarter"), None)),
        check_vma=False,
    )
```
